256 devices in a mesh: dp: 32 (over x_hi, z, core), section: 8 (over y, x_lo).
Axes of the slice: x: 4 (x_hi: 2, x_lo: 2; x = x_hi * 2 + x_lo), y: 4, z: 8, core: 2. Of those that a mesh axis runs over, the one named last changes fastest.
Arguments:
- hidden: bfloat16 [6144, 5120], P('dp', 'section'), may hold values from -450 to 450
- norm_gain: float32 [5120], P('section'), may hold values from 0.5 to 1.5
- kv_weight: bfloat16 [5120, 1024], P('section'), may hold values from -0.078125 to 0.078125
- queries: bfloat16 [6144, 20480], P('dp', 'section'), may hold values from -150 to 150
- out_grad: bfloat16 [6144, 20480], P('dp', 'section'), may hold values from -6 to 6
Outputs:
- query_grad: bfloat16 [6144, 20480], P('dp', 'section')
- kv_weight_grad: float32 [5120, 1024], P('section')
- gain_grad: float32 [5120], P('section')
- normed_grad: bfloat16 [6144, 5120], P('dp', 'section')
The draws below stay inside these ranges and needn't reach their ends.
All inputs are finite; a program needn't handle non-finite values.
Results may differ from the reference program's by a relative error of at most 0.015.
The reference program's roundings to bfloat16 on the way count: a program that leaves them out, or rounds other values in their place, can miss the bound.
Values may be sent and summed in bfloat16 or wider, within the bound.
A program may use at most 64 MiB of HBM per device.

```python
import math
import jax
import jax.numpy as jnp
from jax import lax

D = 5120
HD = 128
KVH = 4
QH = 20
TOK_DEV = 192
TOKENS = 6144
QCOLS = 20480
N_DP = 32
N_SECTION = 8


def draw_hidden(key, part):
    key_row, key_col, key_base = jax.random.split(key, 3)
    row_scale = jnp.exp(jax.random.uniform(key_row, (TOKENS, 1), jnp.float32, 0.0, math.log(10.0)))
    col_index = jnp.arange(D, dtype=jnp.float32) / D
    col_scale = jnp.exp(math.log(3.0) * col_index[None, :] + jax.random.uniform(key_col, (1, D), jnp.float32, 0.0, math.log(10.0 / 3.0)))
    base = jnp.clip(jax.random.normal(key_base, (TOKENS, D), jnp.float32), -4.0, 4.0)
    return (base * row_scale * col_scale).astype(jnp.bfloat16)


def draw_queries(key, part):
    key_base = jax.random.fold_in(key, 0)
    base = jnp.clip(jax.random.normal(key_base, (TOKENS, QCOLS), jnp.float32), -4.0, 4.0)
    return base.astype(jnp.bfloat16)


def block_scale(rng, shape, pieces, smallest, top_value):
    gain, own = 1.0, jax.random.fold_in(rng, 6)
    for position, shards_of in pieces:
        draws = jnp.exp(jax.random.uniform(jax.random.fold_in(own, position), (shards_of,), jnp.float32, smallest / len(pieces), top_value / len(pieces)))
        gain = gain * jnp.repeat(draws, shape[position] // shards_of).reshape([-1 if axis == position else 1 for axis in range(len(shape))])
    return gain


def bell_draw(own_key, dims, deviation, reach, cuts=(), held_as=jnp.bfloat16):
    array = deviation * jax.random.normal(own_key, dims, jnp.float32)
    if cuts:
        array = array * block_scale(own_key, dims, cuts, -0.22, 0.18)
    return jnp.clip(array, -reach, reach).astype(held_as)


def setup_inputs(seed: int = 0) -> dict:
    key_list = jax.random.split(jax.random.key(seed), 6)
    hidden = draw_hidden(jax.random.fold_in(key_list[5], 71), 0)
    norm_gain = jnp.clip(1.0 + 0.1 * jax.random.normal(key_list[1], (D,), jnp.float32), 0.5, 1.5)
    kv_weight = bell_draw(key_list[2], (D, 2 * KVH * HD), D ** -0.5, 0.078125, ((0, 8),))
    queries = draw_queries(jax.random.fold_in(key_list[5], 71), 0)
    out_grad = bell_draw(key_list[4], (TOKENS, QCOLS), 1.0, 6.0, ((0, 32), (1, 8)))
    return dict(hidden=hidden, norm_gain=norm_gain, kv_weight=kv_weight, queries=queries, out_grad=out_grad)


EPSILON = 1e-05

def attend(query_layer, key_rows, value_rows, grad_layer):
    tok_rows = query_layer.shape[0]
    group_size = QH // KVH
    score_scale = HD ** (-0.5)
    query_pos = lax.broadcasted_iota(jnp.int32, (tok_rows, tok_rows), 0)
    key_pos = lax.broadcasted_iota(jnp.int32, (tok_rows, tok_rows), 1)
    causal = key_pos <= query_pos
    query_parts = []
    key_parts = []
    value_parts = []
    for kv_head in range(KVH):
        first_col = kv_head * group_size * HD
        last_col = first_col + group_size * HD
        q_block = query_layer[:, first_col:last_col].reshape(tok_rows, group_size, HD).astype(jnp.float32)
        g_block = grad_layer[:, first_col:last_col].reshape(tok_rows, group_size, HD).astype(jnp.float32)
        k_block = key_rows[:, kv_head * HD:(kv_head + 1) * HD].astype(jnp.float32)
        v_block = value_rows[:, kv_head * HD:(kv_head + 1) * HD].astype(jnp.float32)
        scores = jnp.einsum('qhd,kd->hqk', q_block, k_block) * score_scale
        scores = jnp.where(causal[None], scores, -1e+30)
        row_max = lax.optimization_barrier(jnp.max(scores, axis=2, keepdims=True))
        weights = jnp.exp(scores - row_max)
        attn_prob = weights / lax.optimization_barrier(jnp.sum(weights, axis=2, keepdims=True))
        prob_low = attn_prob.astype(jnp.bfloat16).astype(jnp.float32)
        value_parts.append(jnp.einsum('hqk,qhd->kd', prob_low, g_block))
        prob_grad = jnp.einsum('qhd,kd->hqk', g_block, v_block)
        row_inner = lax.optimization_barrier(jnp.sum(attn_prob * prob_grad, axis=2, keepdims=True))
        score_grad = (attn_prob * (prob_grad - row_inner)).astype(jnp.bfloat16).astype(jnp.float32)
        query_part = jnp.einsum('hqk,kd->qhd', score_grad, k_block) * score_scale
        query_parts.append(query_part.reshape(tok_rows, group_size * HD).astype(jnp.bfloat16))
        key_parts.append(jnp.einsum('hqk,qhd->kd', score_grad, q_block) * score_scale)
    return (jnp.concatenate(query_parts, axis=1), jnp.concatenate(key_parts, axis=1), jnp.concatenate(value_parts, axis=1))

def reference(hidden, norm_gain, kv_weight, queries, out_grad):
    half_cols = KVH * HD
    layer_cols = QH * HD
    hidden_rep = hidden.reshape(N_DP, TOK_DEV, D)
    query_rep = queries.reshape(N_DP, TOK_DEV, N_SECTION, layer_cols).transpose(0, 2, 1, 3)
    grad_rep = out_grad.reshape(N_DP, TOK_DEV, N_SECTION, layer_cols).transpose(0, 2, 1, 3)

    def one_replica(carry, inputs):
        hidden_one, query_one, grad_one = inputs
        hidden_f = hidden_one.astype(jnp.float32)
        inv_rms = lax.rsqrt(lax.optimization_barrier(jnp.sum(hidden_f * hidden_f, axis=1)) / D + EPSILON)
        normed = (hidden_f * inv_rms[:, None] * norm_gain[None, :]).astype(jnp.bfloat16)
        kv_all = jnp.dot(normed, kv_weight, preferred_element_type=jnp.float32).astype(jnp.bfloat16)
        key_rows = kv_all[:, :half_cols]
        value_rows = kv_all[:, half_cols:]

        def layer_step(total, layer_in):
            query_layer, grad_layer = layer_in
            query_part, key_part, value_part = attend(query_layer, key_rows, value_rows, grad_layer)
            return (total + jnp.concatenate([key_part, value_part], axis=1), query_part)
        grad_total, query_grads = lax.scan(layer_step, jnp.zeros((TOK_DEV, 2 * half_cols), jnp.float32), (query_one, grad_one))
        kv_grad = grad_total.astype(jnp.bfloat16)
        weight_term = jnp.dot(normed.T, kv_grad, preferred_element_type=jnp.float32)
        normed_full = jnp.dot(kv_grad, kv_weight.T, preferred_element_type=jnp.float32)
        gain_term = lax.optimization_barrier(jnp.sum(normed_full * hidden_f * inv_rms[:, None], axis=0))
        weight_acc, gain_acc = carry
        query_flat = query_grads.transpose(1, 0, 2).reshape(TOK_DEV, N_SECTION * layer_cols)
        return ((weight_acc + weight_term, gain_acc + gain_term), (query_flat, normed_full.astype(jnp.bfloat16)))
    start = (jnp.zeros((D, 2 * half_cols), jnp.float32), jnp.zeros((D,), jnp.float32))
    (weight_acc, gain_acc), (query_grad, normed_grad) = lax.scan(one_replica, start, (hidden_rep, query_rep, grad_rep))
    return (query_grad.reshape(TOKENS, N_SECTION * layer_cols), weight_acc / N_DP, gain_acc / N_DP, normed_grad.reshape(TOKENS, D))
```

```python
import jax
import jax.numpy as jnp
from jax import lax
from jax.experimental import pallas as pl
from jax.experimental.pallas import tpu as pltpu
from jax.sharding import PartitionSpec as P

D = 5120
HD = 128
KVH = 4
QH = 20
GRP = QH // KVH
NSEC = 8
NZ = 8
TOK = 192
FEAT = 640
HALF = FEAT // 2
RB = 48
EPSILON = 1e-05
SCALE = HD ** (-0.5)
MESH = pl.DeviceIdType.MESH
F32 = jnp.float32
BF16 = jnp.bfloat16

NT = (((1,), (1,)), ((), ()))
NN = (((1,), (0,)), ((), ()))
TN = (((0,), (0,)), ((), ()))


def dot(a, b, dims=NN):
    return lax.dot_general(a, b, dims, preferred_element_type=F32)


def fused_kernel(
    h_hbm, gain_hbm, w_hbm, q_hbm, g_hbm,
    qg_out, wg_out, gg_out, ng_out,
    h_v, gain_v, w_v, q_v, g_v, qg_v, ng_v,
    ss, nrm, nT, nTp,
    part_a, rs_a, kvb, part_b, rs_b, kvg, kvgp,
    pbuf_a, dsbuf_a, pbuf_b, dsbuf_b, nf,
    wp, rz, xs, xr, wgb, gpair, gz, gx,
    loc, out_sem,
    ss_s, ss_r, nt_s, nt_r,
    ra_s, ra_r, aa_s, aa_r, rb_s, rb_r, ab_s, ab_r,
    kp_s, kp_r, rz_s, rz_r, x_s, x_r, az_s, az_r, cc_s, cc_r,
    gp_s, gp_r, gz_s, gz_r, gx_s, gx_r,
):
    dp = lax.axis_index("dp")
    sec = lax.axis_index("section")
    core = lax.rem(dp, 2)
    zz = lax.rem(lax.div(dp, 2), NZ)
    xh = lax.div(dp, 2 * NZ)
    yy = lax.div(sec, 2)
    xl = lax.rem(sec, 2)

    def dp_of(x_, z_, c_):
        return x_ * (2 * NZ) + z_ * 2 + c_

    sec_peer = [None] + [lax.rem(sec + o, NSEC) for o in range(1, NSEC)]
    z_at = [lax.rem(zz + o, NZ) for o in range(NZ)]
    sec_dev = [None] + [(dp, sec_peer[o]) for o in range(1, NSEC)]
    z_dev = [None] + [(dp_of(xh, z_at[o], core), sec) for o in range(1, NZ)]
    core_dev = (dp_of(xh, zz, 1 - core), sec)
    x_dev = (dp_of(1 - xh, zz, core), sec)

    def rcopy(src, dst, s, r, dev):
        return pltpu.make_async_remote_copy(
            src_ref=src, dst_ref=dst, send_sem=s, recv_sem=r, device_id=dev, device_id_type=MESH
        )

    pend = []

    loads = [
        pltpu.make_async_copy(src, dst, loc.at[i])
        for i, (src, dst) in enumerate(
            [(h_hbm, h_v), (gain_hbm, gain_v), (w_hbm, w_v), (q_hbm, q_v), (g_hbm, g_v)]
        )
    ]
    for c in loads:
        c.start()
    bar = pltpu.get_barrier_semaphore()
    partners = sec_dev[1:] + z_dev[1:] + [core_dev, x_dev]
    for dev in partners:
        pl.semaphore_signal(bar, inc=1, device_id=dev, device_id_type=MESH)

    loads[0].wait()
    acc = None
    for t in range(5):
        ht = h_v[:, t * 128:(t + 1) * 128].astype(F32)
        acc = ht * ht if acc is None else acc + ht * ht
    row = jnp.sum(acc.T, axis=0, keepdims=True)
    ss[0] = jnp.broadcast_to(row, (8, TOK))
    pl.semaphore_wait(bar, len(partners))
    ss_c = [
        rcopy(ss.at[0], ss.at[o], ss_s.at[o - 1], ss_r.at[o - 1], sec_dev[o]) for o in range(1, NSEC)
    ]
    for c in ss_c:
        c.start()
    loads[1].wait()
    loads[2].wait()
    for c in ss_c:
        c.wait()
    tot = ss[0]
    for o in range(1, NSEC):
        tot = tot + ss[o]
    inv_row = lax.rsqrt(tot[0:1, :] / D + EPSILON)
    inv = jnp.broadcast_to(inv_row, (128, TOK)).T
    for t in range(5):
        cols = slice(t * 128, (t + 1) * 128)
        n_t = (h_v[:, cols].astype(F32) * inv * gain_v[:, cols]).astype(BF16)
        nrm[:, cols] = n_t
        nT[cols, :] = n_t.T

    ra_c = {}
    for j in range(KVH):
        wj = jnp.concatenate(
            [w_v[:, j * 128:(j + 1) * 128], w_v[:, 512 + j * 128:512 + (j + 1) * 128]], axis=1
        )
        pj = dot(nrm[...], wj)
        part_a[j, 0] = pj[:, 0:128]
        part_a[j, 1] = pj[:, 128:256]
        for o in range(1, NSEC):
            d = sec_peer[o]
            c = rcopy(
                part_a.at[j, lax.rem(d, 2), pl.ds(pl.multiple_of(lax.div(d, 2) * RB, RB), RB), :],
                rs_a.at[j, o - 1], ra_s.at[j, o - 1], ra_r.at[j, o - 1], sec_dev[o],
            )
            c.start()
            ra_c[j, o] = c
    other = pl.multiple_of((1 - core) * HALF, 16)
    nt_c = rcopy(nT.at[pl.ds(other, HALF), :], nTp, nt_s.at[0], nt_r.at[0], core_dev)
    nt_c.start()
    loads[3].wait()
    loads[4].wait()
    my_rows = pl.ds(pl.multiple_of(yy * RB, RB), RB)

    ag = {}

    def reduce_and_gather(j, copies, part, rs, dst, s, r, tag):
        tot = part[j, xl, my_rows, :]
        for o in range(1, NSEC):
            copies[j, o].wait()
        for o in range(1, NSEC):
            tot = tot + rs[j, o - 1]
        dst[j, xl, my_rows, :] = tot.astype(BF16)
        for o in range(1, NSEC):
            piece = dst.at[j, xl, my_rows, :]
            c = rcopy(piece, piece, s.at[j, o - 1], r.at[j, o - 1], sec_dev[o])
            c.start()
            ag[tag, j, o] = c

    def wait_gather(j, tag):
        for o in range(1, NSEC):
            ag[tag, j, o].wait()

    def do_r(j):
        reduce_and_gather(j, ra_c, part_a, rs_a, kvb, aa_s, aa_r, "a")

    mask_a = (
        lax.broadcasted_iota(jnp.int32, (128, 128), 0)
        <= lax.broadcasted_iota(jnp.int32, (128, 128), 1)
    )
    qpos = lax.broadcasted_iota(jnp.int32, (64, 128), 1)
    mask_b = lax.broadcasted_iota(jnp.int32, (64, 128), 0) <= jnp.where(qpos < 64, qpos, qpos - 64)
    rb_c = {}
    qg_c = {}

    def soft(s, dpr):
        m = jnp.max(s, axis=0, keepdims=True)
        e = jnp.exp(s - m)
        p = e * (1.0 / jnp.sum(e, axis=0, keepdims=True))
        inner = jnp.sum(p * dpr, axis=0, keepdims=True)
        return p.astype(BF16), (p * (dpr - inner)).astype(BF16)

    def do_t(j):
        wait_gather(j, "a")
        k = kvb[j, 0]
        v = kvb[j, 1]
        k_lo = k[0:128]
        v_lo = v[0:128]
        col0 = j * GRP * HD

        def heads(ref, rows, hs):
            return [ref[rows, col0 + h * HD:col0 + (h + 1) * HD] for h in hs]

        lo, hi = slice(0, 128), slice(128, TOK)
        for h in range(GRP):
            qh = heads(q_v, lo, [h])[0]
            gh = heads(g_v, lo, [h])[0]
            s = jnp.where(mask_a, dot(k_lo, qh, NT) * SCALE, -1e30)
            p, ds = soft(s, dot(v_lo, gh, NT))
            pbuf_a[:, h * 128:(h + 1) * 128] = p
            dsbuf_a[:, h * 128:(h + 1) * 128] = ds
        q_hi = jnp.concatenate(heads(q_v, hi, range(GRP)) + heads(q_v, hi, [GRP - 1]), axis=0)
        g_hi = jnp.concatenate(heads(g_v, hi, range(GRP)) + heads(g_v, hi, [GRP - 1]), axis=0)
        for i in range(3):
            qh = q_hi[i * 128:(i + 1) * 128]
            gh = g_hi[i * 128:(i + 1) * 128]
            s = dot(k, qh, NT) * SCALE
            s = jnp.concatenate([s[0:128], jnp.where(mask_b, s[128:TOK], -1e30)], axis=0)
            p, ds = soft(s, dot(v, gh, NT))
            pbuf_b[:, i * 128:(i + 1) * 128] = p
            dsbuf_b[:, i * 128:(i + 1) * 128] = ds
        q_lo = jnp.concatenate(heads(q_v, lo, range(GRP)), axis=0)
        g_lo = jnp.concatenate(heads(g_v, lo, range(GRP)), axis=0)
        nb = 64 * GRP
        kb = dot(dsbuf_b[:, 0:nb], q_hi[0:nb])
        vb = dot(pbuf_b[:, 0:nb], g_hi[0:nb])
        ka = dot(dsbuf_a[...], q_lo)
        va = dot(pbuf_a[...], g_lo)
        part_b[j, 0, 0:128] = (ka + kb[0:128]) * SCALE
        part_b[j, 0, 128:TOK] = kb[128:TOK] * SCALE
        part_b[j, 1, 0:128] = va + vb[0:128]
        part_b[j, 1, 128:TOK] = vb[128:TOK]
        for o in range(1, NSEC):
            d = sec_peer[o]
            c = rcopy(
                part_b.at[j, lax.rem(d, 2), pl.ds(pl.multiple_of(lax.div(d, 2) * RB, RB), RB), :],
                rs_b.at[j, o - 1], rb_s.at[j, o - 1], rb_r.at[j, o - 1], sec_dev[o],
            )
            c.start()
            rb_c[j, o] = c
        qa = dot(dsbuf_a[...], k_lo, TN) * SCALE
        qb = dot(dsbuf_b[:, 0:nb], k, TN) * SCALE
        for h in range(GRP):
            qg_v[0:128, col0 + h * HD:col0 + (h + 1) * HD] = qa[h * 128:(h + 1) * 128].astype(BF16)
            qg_v[128:TOK, col0 + h * HD:col0 + (h + 1) * HD] = qb[h * 64:(h + 1) * 64].astype(BF16)
        c = pltpu.make_async_copy(
            qg_v.at[:, col0:col0 + GRP * HD], qg_out.at[:, col0:col0 + GRP * HD], out_sem.at[j]
        )
        c.start()
        qg_c[j] = c

    def do_u(j):
        reduce_and_gather(j, rb_c, part_b, rs_b, kvg, ab_s, ab_r, "b")

    kp_c = {}

    def do_x(j):
        wait_gather(j, "b")
        c = rcopy(kvg.at[j], kvgp.at[j], kp_s.at[j], kp_r.at[j], core_dev)
        c.start()
        kp_c[j] = c

    def ring(j, d):
        sign = 1 if d == 0 else -1
        hops = 4 if (j + d) % 2 == 0 else 3
        slot0 = 0 if d == 0 else 4
        return sign, hops, slot0

    rz_c = {}

    def send_ring(j, d, s):
        sign, hops, slot0 = ring(j, d)
        chunk = z_at[(sign * (hops - s)) % NZ]
        if s == 0:
            src = wp.at[j, chunk]
        else:
            rz_c[j, d, s - 1].wait()
            rz[j, slot0 + s - 1] = rz[j, slot0 + s - 1] + wp[j, chunk]
            src = rz.at[j, slot0 + s - 1]
        c = rcopy(
            src, rz.at[j, slot0 + s], rz_s.at[j, slot0 + s], rz_r.at[j, slot0 + s], z_dev[sign % NZ]
        )
        c.start()
        rz_c[j, d, s] = c

    def do_y(j):
        if j == 0:
            nt_c.wait()
        kp_c[j].wait()
        mine = pl.ds(pl.multiple_of(core * HALF, 16), HALF)
        both = jnp.concatenate([kvg[j, 0], kvg[j, 1]], axis=1)
        both_p = jnp.concatenate([kvgp[j, 0], kvgp[j, 1]], axis=1)
        prod = dot(nT[mine, :], both) + dot(nTp[...], both_p)
        for r in range(4):
            for cb in range(2):
                wp[j, 2 * r + cb] = prod[r * 80:(r + 1) * 80, cb * 128:(cb + 1) * 128]
        send_ring(j, 0, 0)
        send_ring(j, 1, 0)

    def do_nf(j):
        both = jnp.concatenate([kvg[j, 0], kvg[j, 1]], axis=1)
        wj = jnp.concatenate(
            [w_v[:, j * 128:(j + 1) * 128], w_v[:, 512 + j * 128:512 + (j + 1) * 128]], axis=1
        )
        term = dot(both, wj, NT)
        nf[...] = term if j == 0 else nf[...] + term

    g_c = {}

    def do_gain():
        gpair[0] = jnp.zeros((8, 128), F32)
        for t in range(5):
            cols = slice(t * 128, (t + 1) * 128)
            full = nf[:, cols]
            ng_v[:, cols] = full.astype(BF16)
            term = full * h_v[:, cols].astype(F32) * inv
            gpair[0, t:t + 1, :] = jnp.sum(term, axis=0, keepdims=True)
        c = rcopy(gpair.at[0], gpair.at[1], gp_s.at[0], gp_r.at[0], core_dev)
        c.start()
        g_c["p"] = c
        c = pltpu.make_async_copy(ng_v, ng_out, out_sem.at[4])
        c.start()
        g_c["ng"] = c

    def do_gain_z():
        g_c["p"].wait()
        gz[zz] = gpair[0] + gpair[1]
        for o in range(1, NZ):
            c = rcopy(gz.at[zz], gz.at[zz], gz_s.at[o - 1], gz_r.at[o - 1], z_dev[o])
            c.start()
            g_c[o] = c

    def do_gain_x():
        for o in range(1, NZ):
            g_c[o].wait()
        tot = gz[0]
        for i in range(1, NZ):
            tot = tot + gz[i]
        gx[0] = tot
        c = rcopy(gx.at[0], gx.at[1], gx_s.at[0], gx_r.at[0], x_dev)
        c.start()
        g_c["x"] = c

    def do_gain_end():
        g_c["x"].wait()
        gx[2] = (gx[0] + gx[1]) * (1.0 / 32.0)
        c = pltpu.make_async_copy(gx.at[2], gg_out, out_sem.at[5])
        c.start()
        g_c["out"] = c

    def do_z(j, s):
        for d in range(2):
            if s < ring(j, d)[1]:
                send_ring(j, d, s)

    x_c = {}

    def do_xx(j):
        tot = wp[j, zz]
        for d in range(2):
            _, hops, slot0 = ring(j, d)
            rz_c[j, d, hops - 1].wait()
            tot = tot + rz[j, slot0 + hops - 1]
        xs[j] = tot
        c = rcopy(xs.at[j], xr.at[j], x_s.at[j], x_r.at[j], x_dev)
        c.start()
        x_c[j] = c

    az_c = {}

    def fwd(j, d, s):
        sign, hops, slot0 = ring(j, d)
        if s > 0:
            az_c[j, d, s - 1].wait()
        if s < hops:
            chunk = z_at[(-sign * s) % NZ]
            piece = wgb.at[core, j, chunk]
            c = rcopy(piece, piece, az_s.at[j, slot0 + s], az_r.at[j, slot0 + s], z_dev[sign % NZ])
            c.start()
            az_c[j, d, s] = c

    def do_g(j, s):
        if s == 0:
            x_c[j].wait()
            wgb[core, j, zz] = ((xs[j] + xr[j]) * (1.0 / 32.0)).astype(BF16)
        for d in range(2):
            if s <= ring(j, d)[1]:
                fwd(j, d, s)

    cc_c = {}

    def do_cc(j):
        piece = wgb.at[core, j]
        c = rcopy(piece, piece, cc_s.at[j], cc_r.at[j], core_dev)
        c.start()
        cc_c[j] = c

    wo_c = {}

    def do_out(j):
        cc_c[j].wait()
        for half in range(2):
            c = pltpu.make_async_copy(wgb.at[half, j], wg_out.at[half, j], out_sem.at[6 + 2 * j + half])
            c.start()
            wo_c[j, half] = c

    tasks = []
    for j in range(KVH):
        tasks.append((5.4 + 2.1 * j, do_r, (j,)))
        tasks.append((9.7 + 2.1 * j, do_t, (j,)))
        b0 = 17.0 + 3.0 * j
        tasks.append((b0, do_u, (j,)))
        tasks.append((b0 + 4.4, do_x, (j,)))
        tasks.append((b0 + 5.7, do_y, (j,)))
        tasks.append((b0 + 5.8, do_nf, (j,)))
        for s in range(1, 4):
            tasks.append((b0 + 5.7 + 2.6 * s, do_z, (j, s)))
        tasks.append((b0 + 16.1, do_xx, (j,)))
        for s in range(0, 5):
            tasks.append((b0 + 18.6 + 2.2 * s, do_g, (j, s)))
        tasks.append((b0 + 27.5, do_cc, (j,)))
        tasks.append((b0 + 28.8, do_out, (j,)))
    last = 17.0 + 3.0 * 3
    tasks.append((last + 5.9, do_gain, ()))
    tasks.append((last + 8.4, do_gain_z, ()))
    tasks.append((last + 13.5, do_gain_x, ()))
    tasks.append((last + 18.5, do_gain_end, ()))
    tasks.sort(key=lambda t: t[0])
    for _, f, a in tasks:
        f(*a)

    for j in range(KVH):
        qg_c[j].wait()
        for half in range(2):
            wo_c[j, half].wait()
    g_c["ng"].wait()
    g_c["out"].wait()


def finish_kernel(wgb_ref, out_ref):
    for r in range(4):
        for cb in range(2):
            out_ref[r * 80:(r + 1) * 80, cb * 512:(cb + 1) * 512] = jnp.concatenate(
                [wgb_ref[0, j, 2 * r + cb].astype(F32) for j in range(KVH)], axis=1
            )


def shards(hidden, norm_gain, kv_weight, queries, out_grad):
    any_spec = pl.BlockSpec(memory_space=pl.ANY)
    dma = pltpu.SemaphoreType.DMA
    vm = pltpu.VMEM
    scratch = [
        vm((TOK, FEAT), BF16), vm((1, FEAT), F32), vm((FEAT, 1024), BF16),
        vm((TOK, QH * HD), BF16), vm((TOK, QH * HD), BF16), vm((TOK, QH * HD), BF16), vm((TOK, FEAT), BF16),
        vm((NSEC, 8, TOK), F32), vm((TOK, FEAT), BF16), vm((FEAT, TOK), BF16), vm((HALF, TOK), BF16),
        vm((KVH, 2, TOK, HD), F32), vm((KVH, 7, RB, HD), F32), vm((KVH, 2, TOK, HD), BF16),
        vm((KVH, 2, TOK, HD), F32), vm((KVH, 7, RB, HD), F32), vm((KVH, 2, TOK, HD), BF16),
        vm((KVH, 2, TOK, HD), BF16),
        vm((128, 640), BF16), vm((128, 640), BF16), vm((TOK, 384), BF16), vm((TOK, 384), BF16),
        vm((TOK, FEAT), F32),
        vm((KVH, NZ, 80, 128), F32), vm((KVH, 8, 80, 128), F32), vm((KVH, 80, 128), F32),
        vm((KVH, 80, 128), F32), vm((2, KVH, NZ, 80, 128), BF16),
        vm((2, 8, 128), F32), vm((NZ, 8, 128), F32), vm((3, 8, 128), F32),
        dma((5,)), dma((14,)),
        dma((7,)), dma((7,)), dma((1,)), dma((1,)),
        dma((KVH, 7)), dma((KVH, 7)), dma((KVH, 7)), dma((KVH, 7)),
        dma((KVH, 7)), dma((KVH, 7)), dma((KVH, 7)), dma((KVH, 7)),
        dma((KVH,)), dma((KVH,)), dma((KVH, 8)), dma((KVH, 8)), dma((KVH,)), dma((KVH,)),
        dma((KVH, 8)), dma((KVH, 8)), dma((KVH,)), dma((KVH,)),
        dma((1,)), dma((1,)), dma((7,)), dma((7,)), dma((1,)), dma((1,)),
    ]
    query_grad, wgb, gain8, normed_grad = pl.pallas_call(
        fused_kernel,
        out_shape=(
            jax.ShapeDtypeStruct((TOK, QH * HD), BF16),
            jax.ShapeDtypeStruct((2, KVH, NZ, 80, 128), BF16),
            jax.ShapeDtypeStruct((8, 128), F32),
            jax.ShapeDtypeStruct((TOK, FEAT), BF16),
        ),
        in_specs=[any_spec] * 5,
        out_specs=(any_spec,) * 4,
        scratch_shapes=scratch,
        compiler_params=pltpu.CompilerParams(
            collective_id=0, has_side_effects=True, vmem_limit_bytes=40 * 1024 * 1024
        ),
        name="fused",
    )(hidden, norm_gain.reshape(1, FEAT), kv_weight, queries, out_grad)
    weight_grad = pl.pallas_call(
        finish_kernel,
        grid=(2,),
        out_shape=jax.ShapeDtypeStruct((FEAT, 1024), F32),
        in_specs=[pl.BlockSpec((1, KVH, NZ, 80, 128), lambda i: (i, 0, 0, 0, 0))],
        out_specs=pl.BlockSpec((HALF, 1024), lambda i: (i, 0)),
        name="finish",
    )(wgb)
    return query_grad, weight_grad, gain8[:5].reshape(FEAT), normed_grad


def solution(mesh):
    placed = (
        P("dp", "section"),
        P("section"),
        P("section", None),
        P("dp", "section"),
        P("dp", "section"),
    )
    return jax.shard_map(
        shards,
        mesh=mesh,
        in_specs=placed,
        out_specs=(P("dp", "section"), P("section", None), P("section"), P("dp", "section")),
        check_vma=False,
    )
```

```python
import jax
import jax.numpy as jnp
from jax import lax
from jax.experimental import pallas as pl
from jax.experimental.pallas import tpu as pltpu
from jax.sharding import PartitionSpec as P

D = 5120
HD = 128
KVH = 4
QH = 20
GRP = QH // KVH
NSEC = 8
NZ = 8
TOK = 192
FEAT = 640
HALF = FEAT // 2
RB = 48
AHEAD = 4
DIRECT = (0, 1, 2, 3)
EPSILON = 1e-05
SCALE = HD ** (-0.5)
MESH = pl.DeviceIdType.MESH
F32 = jnp.float32
BF16 = jnp.bfloat16

NT = (((1,), (1,)), ((), ()))
NN = (((1,), (0,)), ((), ()))
TN = (((0,), (0,)), ((), ()))


def dot(a, b, dims=NN):
    return lax.dot_general(a, b, dims, preferred_element_type=F32)


def fused_kernel(
    h_hbm, gain_hbm, w_hbm, q_hbm, g_hbm,
    qg_v, wg_v, gx, ng_v,
    h_v, gain_v, w_v, q_v, g_v,
    ss, ngat,
    part_a, rs_a, st_a, kvb, part_b, rs_b, st_b, kvg, kvt, kvr,
    pbuf_a, dsbuf_a, pbuf_b, dsbuf_b, nf,
    xs, xr, wgb, gpair, gz,
    loc, ss_s, ss_r, ng_s, ng_r, nc_s, nc_r,
    ra_s, ra_r, aa_s, aa_r, rb_s, rb_r, ab_s, ab_r,
    kt_s, ku_s, kt_r, x_s, x_r, az_s, az_r, cc_s, cc_r,
    gp_s, gp_r, gz_s, gz_r, gx_s, gx_r,
):
    dp = lax.axis_index("dp")
    sec = lax.axis_index("section")
    core = lax.rem(dp, 2)
    zz = lax.rem(lax.div(dp, 2), NZ)
    xh = lax.div(dp, 2 * NZ)
    yy = lax.div(sec, 2)
    xl = lax.rem(sec, 2)

    def dp_of(x_, z_, c_):
        return x_ * (2 * NZ) + z_ * 2 + c_

    sec_peer = [None] + [lax.rem(sec + o, NSEC) for o in range(1, NSEC)]
    z_at = [lax.rem(zz + o, NZ) for o in range(NZ)]
    sec_dev = [None] + [(dp, sec_peer[o]) for o in range(1, NSEC)]
    z_dev = [None] + [(dp_of(xh, z_at[o], core), sec) for o in range(1, NZ)]
    z_dev2 = [(dp_of(xh, z_at[o], 1 - core), sec) for o in range(NZ)]
    core_dev = z_dev2[0]
    x_dev = (dp_of(1 - xh, zz, core), sec)

    def rcopy(src, dst, s, r, dev):
        return pltpu.make_async_remote_copy(
            src_ref=src, dst_ref=dst, send_sem=s, recv_sem=r, device_id=dev, device_id_type=MESH
        )

    def wait_bytes(ref, sem):
        pltpu.make_async_copy(ref, ref, sem).wait()

    sends = []

    def start(c):
        c.start()
        sends.append(c.wait_send)

    def send_total(ref, sem):
        sends.append(lambda: wait_bytes(ref, sem))

    loads = [
        pltpu.make_async_copy(src, dst, loc.at[i])
        for i, (src, dst) in enumerate(
            [(h_hbm, h_v), (gain_hbm, gain_v.at[0]), (w_hbm, w_v), (q_hbm, q_v), (g_hbm, g_v)]
        )
    ]
    for c in loads:
        c.start()
    bar = pltpu.get_barrier_semaphore()
    partners = sec_dev[1:] + z_dev[1:] + z_dev2 + [x_dev]
    for dev in partners:
        pl.semaphore_signal(bar, inc=1, device_id=dev, device_id_type=MESH)

    loads[0].wait()
    acc = None
    for t in range(5):
        ht = h_v[:, t * 128:(t + 1) * 128].astype(F32)
        acc = ht * ht if acc is None else acc + ht * ht
    row = jnp.sum(acc.T, axis=0, keepdims=True)
    ss[0] = row
    pl.semaphore_wait(bar, len(partners))
    for o in range(1, NSEC):
        rcopy(ss.at[0], ss.at[o], ss_s.at[0], ss_r.at[0], sec_dev[o]).start()
    send_total(ss.at[1:NSEC], ss_s.at[0])
    loads[1].wait()
    loads[2].wait()
    wait_bytes(ss.at[1:NSEC], ss_r.at[0])
    tot = ss[0]
    for o in range(1, NSEC):
        tot = tot + ss[o]
    inv_row = lax.rsqrt(tot / D + EPSILON)
    inv = jnp.broadcast_to(inv_row, (128, TOK)).T
    for t in range(5):
        cols = slice(t * 128, (t + 1) * 128)
        n_t = (h_v[:, cols].astype(F32) * inv * gain_v[:, cols]).astype(BF16)
        ngat[core, zz, :, cols] = n_t

    my_rows = pl.ds(pl.multiple_of(yy * RB, RB), RB)

    def scatter(j, part, rs, s, r):
        for o in range(1, NSEC):
            d = sec_peer[o]
            rcopy(
                part.at[j, lax.rem(d, 2), pl.ds(pl.multiple_of(lax.div(d, 2) * RB, RB), RB), :],
                rs.at[j, o - 1], s.at[j], r.at[j], sec_dev[o],
            ).start()
        send_total(rs.at[j], s.at[j])

    def reduce_and_gather(j, part, rs, rs_r, st, dst, s, r):
        wait_bytes(rs.at[j], rs_r.at[j])
        tot = part[j, xl, my_rows, :]
        for o in range(1, NSEC):
            tot = tot + rs[j, o - 1]
        st[j] = tot.astype(BF16)
        piece = dst.at[j, xl, my_rows, :]
        for o in range(1, NSEC):
            rcopy(st.at[j], piece, s.at[j], r.at[j], sec_dev[o]).start()
        pltpu.make_async_copy(st.at[j], piece, r.at[j]).start()
        send_total(rs.at[j, :, 0:RB // 2, :], s.at[j])

    def weight_cols(j):
        return jnp.concatenate(
            [w_v[:, j * 128:(j + 1) * 128], w_v[:, 512 + j * 128:512 + (j + 1) * 128]], axis=1
        )

    def do_s(j):
        pj = dot(ngat[core, zz], weight_cols(j))
        part_a[j, 0] = pj[:, 0:128]
        part_a[j, 1] = pj[:, 128:256]
        scatter(j, part_a, rs_a, ra_s, ra_r)

    for j in range(AHEAD):
        do_s(j)
    def ring(j, d):
        sign = 1 if d == 0 else -1
        hops = 4 if (j + d) % 2 == 0 else 3
        slot0 = 0 if d == 0 else (3 if j % 2 else 4)
        return sign, hops, slot0

    ng_c = {}

    def do_ng(s, h):
        rows = pl.ds(h * 96, 96)
        if s == 0:
            own = ngat.at[core, zz, rows]
            rcopy(own, own, nc_s.at[0], nc_r.at[0], core_dev).start()
        for d in range(2):
            sign, hops, slot0 = ring(h, d)
            piece = ngat.at[core, z_at[(-sign * s) % NZ], rows]
            if 0 < s <= hops:
                ng_c[h, d, s - 1].wait_recv()
            if s < hops:
                c = rcopy(piece, piece, ng_s.at[0], ng_r.at[h, slot0 + s], z_dev[sign % NZ])
                c.start()
                ng_c[h, d, s] = c
            if 0 < s <= hops:
                rcopy(piece, piece, nc_s.at[0], nc_r.at[0], core_dev).start()

    do_ng(0, 0)
    do_ng(0, 1)
    send_total(ngat.at[0, 1:NZ], ng_s.at[0])
    send_total(ngat.at[0], nc_s.at[0])
    loads[3].wait()
    loads[4].wait()

    def do_r(j):
        reduce_and_gather(j, part_a, rs_a, ra_r, st_a, kvb, aa_s, aa_r)

    mask_a = (
        lax.broadcasted_iota(jnp.int32, (128, 128), 0)
        <= lax.broadcasted_iota(jnp.int32, (128, 128), 1)
    )
    qpos = lax.broadcasted_iota(jnp.int32, (64, 128), 1)
    mask_b = lax.broadcasted_iota(jnp.int32, (64, 128), 0) <= jnp.where(qpos < 64, qpos, qpos - 64)

    def soft(s, dpr):
        m = jnp.max(s, axis=0, keepdims=True)
        e = jnp.exp(s - m)
        p = e * (1.0 / jnp.sum(e, axis=0, keepdims=True))
        inner = jnp.sum(p * dpr, axis=0, keepdims=True)
        return p.astype(BF16), (p * (dpr - inner)).astype(BF16)

    def do_t(j):
        wait_bytes(kvb.at[j], aa_r.at[j])
        k = kvb[j, 0]
        v = kvb[j, 1]
        k_lo = k[0:128]
        v_lo = v[0:128]
        col0 = j * GRP * HD

        def heads(ref, rows, hs):
            return [ref[rows, col0 + h * HD:col0 + (h + 1) * HD] for h in hs]

        lo, hi = slice(0, 128), slice(128, TOK)
        for h in range(GRP):
            qh = heads(q_v, lo, [h])[0]
            gh = heads(g_v, lo, [h])[0]
            s = jnp.where(mask_a, dot(k_lo, qh, NT) * SCALE, -1e30)
            p, ds = soft(s, dot(v_lo, gh, NT))
            pbuf_a[:, h * 128:(h + 1) * 128] = p
            dsbuf_a[:, h * 128:(h + 1) * 128] = ds
        q_hi = jnp.concatenate(heads(q_v, hi, range(GRP)) + heads(q_v, hi, [GRP - 1]), axis=0)
        g_hi = jnp.concatenate(heads(g_v, hi, range(GRP)) + heads(g_v, hi, [GRP - 1]), axis=0)
        for i in range(3):
            qh = q_hi[i * 128:(i + 1) * 128]
            gh = g_hi[i * 128:(i + 1) * 128]
            s = dot(k, qh, NT) * SCALE
            s = jnp.concatenate([s[0:128], jnp.where(mask_b, s[128:TOK], -1e30)], axis=0)
            p, ds = soft(s, dot(v, gh, NT))
            pbuf_b[:, i * 128:(i + 1) * 128] = p
            dsbuf_b[:, i * 128:(i + 1) * 128] = ds
        q_lo = jnp.concatenate(heads(q_v, lo, range(GRP)), axis=0)
        g_lo = jnp.concatenate(heads(g_v, lo, range(GRP)), axis=0)
        nb = 64 * GRP
        kb = dot(dsbuf_b[:, 0:nb], q_hi[0:nb])
        vb = dot(pbuf_b[:, 0:nb], g_hi[0:nb])
        ka = dot(dsbuf_a[...], q_lo)
        va = dot(pbuf_a[...], g_lo)
        part_b[j, 0, 0:128] = (ka + kb[0:128]) * SCALE
        part_b[j, 0, 128:TOK] = kb[128:TOK] * SCALE
        part_b[j, 1, 0:128] = va + vb[0:128]
        part_b[j, 1, 128:TOK] = vb[128:TOK]
        scatter(j, part_b, rs_b, rb_s, rb_r)
        qa = dot(dsbuf_a[...], k_lo, TN) * SCALE
        qb = dot(dsbuf_b[:, 0:nb], k, TN) * SCALE
        for h in range(GRP):
            qg_v[0:128, col0 + h * HD:col0 + (h + 1) * HD] = qa[h * 128:(h + 1) * 128].astype(BF16)
            qg_v[128:TOK, col0 + h * HD:col0 + (h + 1) * HD] = qb[h * 64:(h + 1) * 64].astype(BF16)

    def do_u(j):
        reduce_and_gather(j, part_b, rs_b, rb_r, st_b, kvg, ab_s, ab_r)

    def do_x(j):
        wait_bytes(kvg.at[j], ab_r.at[j])
        for kv in range(2):
            turned = kvg[j, kv].T
            for z in range(NZ):
                kvt[j, kv, z] = turned[z * 16:(z + 1) * 16]
        slot = kvr.at[j, core, zz]
        for o in range(1, NZ):
            rcopy(kvt.at[j, core, z_at[o]], slot, kt_s.at[j], kt_r.at[j], z_dev[o]).start()
        for o in range(NZ):
            rcopy(kvt.at[j, 1 - core, z_at[o]], slot, ku_s.at[j], kt_r.at[j], z_dev2[o]).start()
        pltpu.make_async_copy(kvt.at[j, core, zz], slot, kt_r.at[j]).start()
        send_total(kvr.at[j, 0, 1:NZ], kt_s.at[j])
        send_total(kvr.at[j, 0], ku_s.at[j])

    x_c = {}

    def do_k(j):
        if j == 0:
            wait_bytes(ngat.at[0], nc_r.at[0])
        wait_bytes(kvr.at[j], kt_r.at[j])
        tot = None
        for c in range(2):
            for z in range(NZ):
                term = dot(kvr[j, c, z], ngat[c, z])
                tot = term if tot is None else tot + term
        xs[j] = tot
        c = rcopy(xs.at[j], xr.at[j], x_s.at[j], x_r.at[j], x_dev)
        start(c)
        x_c[j] = c

    def do_nf(j):
        both = jnp.concatenate([kvg[j, 0], kvg[j, 1]], axis=1)
        term = dot(both, weight_cols(j), NT)
        nf[...] = term if j == 0 else nf[...] + term

    def do_gain():
        gpair[0] = jnp.zeros((8, 128), F32)
        for t in range(5):
            cols = slice(t * 128, (t + 1) * 128)
            full = nf[:, cols]
            ng_v[:, cols] = full.astype(BF16)
            term = full * h_v[:, cols].astype(F32) * inv
            gpair[0, t:t + 1, :] = jnp.sum(term, axis=0, keepdims=True)
        c = rcopy(gpair.at[0], gpair.at[1], gp_s.at[0], gp_r.at[0], core_dev)
        start(c)
        g_c["p"] = c

    g_c = {}

    def do_gain_z():
        g_c["p"].wait_recv()
        gz[zz] = gpair[0] + gpair[1]
        for o in range(1, NZ):
            rcopy(gz.at[zz], gz.at[zz], gz_s.at[0], gz_r.at[0], z_dev[o]).start()
        send_total(gz.at[1:NZ], gz_s.at[0])

    def do_gain_x():
        wait_bytes(gz.at[1:NZ], gz_r.at[0])
        tot = gz[0]
        for i in range(1, NZ):
            tot = tot + gz[i]
        gpair[2] = tot
        c = rcopy(gpair.at[2], gpair.at[3], gx_s.at[0], gx_r.at[0], x_dev)
        start(c)
        g_c["x"] = c

    def do_gain_end():
        g_c["x"].wait_recv()
        gx[...] = (gpair[2] + gpair[3]) * (1.0 / 32.0)

    az_c = {}

    def do_g(j):
        x_c[j].wait_recv()
        wgb[core, j, zz] = ((xs[j] + xr[j]) * (1.0 / 32.0)).astype(BF16)
        if j in DIRECT:
            piece = wgb.at[core, j, zz]
            for o in range(1, NZ):
                rcopy(piece, piece, az_s.at[j], az_r.at[j, 0], z_dev[o]).start()
        else:
            do_a(j, 0)
        send_total(wgb.at[0, j, 1:NZ], az_s.at[j])

    def do_a(j, s):
        for d in range(2):
            sign, hops, slot0 = ring(j, d)
            if 0 < s <= hops:
                az_c[j, d, s - 1].wait_recv()
            if s < hops:
                chunk = z_at[(-sign * s) % NZ]
                piece = wgb.at[core, j, chunk]
                c = rcopy(piece, piece, az_s.at[j], az_r.at[j, slot0 + s], z_dev[sign % NZ])
                c.start()
                az_c[j, d, s] = c

    cc_c = {}

    def do_cc(j):
        if j in DIRECT:
            wait_bytes(wgb.at[0, j, 1:NZ], az_r.at[j, 0])
        piece = wgb.at[core, j]
        c = rcopy(piece, piece, cc_s.at[j], cc_r.at[j], core_dev)
        start(c)
        cc_c[j] = c

    def do_out(j):
        cc_c[j].wait_recv()
        for half in range(2):
            wide = wgb[half, j].astype(F32).reshape(128, FEAT)
            wg_v[:, half * 512 + j * 128:half * 512 + (j + 1) * 128] = wide.T

    R, T, U, X, N, H = do_r, do_t, do_u, do_x, do_nf, do_ng
    K, G, A, C, O = do_k, do_g, do_a, do_cc, do_out
    steps = [
        (R, 0), (H, 1, 0), (R, 1), (H, 1, 1), (R, 2), (H, 2, 0), (R, 3), (T, 0), (H, 2, 1), (T, 1), (T, 2),
        (H, 3, 0), (T, 3), (H, 3, 1), (U, 0), (U, 1), (H, 4, 0), (U, 2), (U, 3), (H, 4, 1),
        (X, 0), (X, 1), (X, 2), (X, 3), (N, 0), (N, 1), (N, 2), (N, 3),
        (do_gain,), (K, 0), (do_gain_z,), (K, 1), (G, 0), (K, 2), (G, 1), (K, 3), (do_gain_x,),
        (G, 2), (G, 3), (C, 0), (C, 1), (O, 0), (do_gain_end,), (C, 2), (O, 1), (C, 3), (O, 2), (O, 3),
    ]
    for step in steps:
        step[0](*step[1:])

    for wait in sends:
        wait()


def finish_kernel(qg, wg, gx, ng, qg_out, wg_out, gg_out, ng_out, sem):
    copies = [(wg.at[i * 80:(i + 1) * 80], wg_out.at[i * 80:(i + 1) * 80]) for i in range(8)]
    copies += [(qg.at[i * 48:(i + 1) * 48], qg_out.at[i * 48:(i + 1) * 48]) for i in range(4)]
    copies += [(ng, ng_out)]
    copies += [(gx.at[t], gg_out.at[t * 128:(t + 1) * 128]) for t in range(5)]
    copies = [pltpu.make_async_copy(a, b, sem.at[i]) for i, (a, b) in enumerate(copies)]
    for c in copies:
        c.start()
    for c in copies:
        c.wait()


def shards(hidden, norm_gain, kv_weight, queries, out_grad):
    hbm = pl.BlockSpec(memory_space=pltpu.HBM)
    in_vmem = pl.BlockSpec(memory_space=pltpu.VMEM)
    dma = pltpu.SemaphoreType.DMA
    vm = pltpu.VMEM
    scratch = [
        vm((TOK, FEAT), BF16), vm((1, FEAT), F32), vm((FEAT, 1024), BF16),
        vm((TOK, QH * HD), BF16), vm((TOK, QH * HD), BF16),
        vm((NSEC, 1, TOK), F32), vm((2, NZ, TOK, FEAT), BF16),
        vm((KVH, 2, TOK, HD), F32), vm((KVH, 7, RB, HD), F32), vm((KVH, RB, HD), BF16),
        vm((KVH, 2, TOK, HD), BF16),
        vm((KVH, 2, TOK, HD), F32), vm((KVH, 7, RB, HD), F32), vm((KVH, RB, HD), BF16),
        vm((KVH, 2, TOK, HD), BF16), vm((KVH, 2, NZ, 16, TOK), BF16), vm((KVH, 2, NZ, 16, TOK), BF16),
        vm((128, 640), BF16), vm((128, 640), BF16), vm((TOK, 384), BF16), vm((TOK, 384), BF16),
        vm((TOK, FEAT), F32),
        vm((KVH, 16, FEAT), F32), vm((KVH, 16, FEAT), F32), vm((2, KVH, NZ, 16, FEAT), BF16),
        vm((4, 8, 128), F32), vm((NZ, 8, 128), F32),
        dma((5,)), dma((1,)), dma((1,)), dma((1,)), dma((2, 7)), dma((1,)), dma((1,)),
        dma((KVH,)), dma((KVH,)), dma((KVH,)), dma((KVH,)),
        dma((KVH,)), dma((KVH,)), dma((KVH,)), dma((KVH,)),
        dma((KVH,)), dma((KVH,)), dma((KVH,)), dma((KVH,)), dma((KVH,)),
        dma((KVH,)), dma((KVH, 7)), dma((KVH,)), dma((KVH,)),
        dma((1,)), dma((1,)), dma((1,)), dma((1,)), dma((1,)), dma((1,)),
    ]
    held = pl.pallas_call(
        fused_kernel,
        out_shape=(
            vm((TOK, QH * HD), BF16),
            vm((FEAT, 1024), F32),
            vm((8, 128), F32),
            vm((TOK, FEAT), BF16),
        ),
        in_specs=[hbm] * 5,
        out_specs=(in_vmem,) * 4,
        scratch_shapes=scratch,
        compiler_params=pltpu.CompilerParams(
            collective_id=0, has_side_effects=True, vmem_limit_bytes=40 * 1024 * 1024
        ),
        name="fused",
    )(*[pltpu.with_memory_space_constraint(a, pltpu.HBM) for a in (hidden, norm_gain, kv_weight, queries, out_grad)])
    query_grad, weight_grad, gain_grad, normed_grad = pl.pallas_call(
        finish_kernel,
        out_shape=(
            jax.ShapeDtypeStruct((TOK, QH * HD), BF16),
            jax.ShapeDtypeStruct((FEAT, 1024), F32),
            jax.ShapeDtypeStruct((FEAT,), F32),
            jax.ShapeDtypeStruct((TOK, FEAT), BF16),
        ),
        in_specs=[in_vmem] * 4,
        out_specs=(hbm,) * 4,
        scratch_shapes=[dma((18,))],
        compiler_params=pltpu.CompilerParams(vmem_limit_bytes=1024 * 1024),
        name="finish",
    )(*[pltpu.with_memory_space_constraint(a, pltpu.VMEM) for a in held])
    return query_grad, weight_grad, gain_grad, normed_grad


def solution(mesh):
    placed = (
        P("dp", "section"),
        P("section"),
        P("section", None),
        P("dp", "section"),
        P("dp", "section"),
    )
    return jax.shard_map(
        shards,
        mesh=mesh,
        in_specs=placed,
        out_specs=(P("dp", "section"), P("section", None), P("section"), P("dp", "section")),
        check_vma=False,
    )
```

```python
import jax
import jax.numpy as jnp
from jax import lax
from jax.experimental import pallas as pl
from jax.experimental.pallas import tpu as pltpu
from jax.sharding import PartitionSpec as P

D = 5120
HD = 128
KVH = 4
QH = 20
GRP = QH // KVH
NSEC = 8
NZ = 8
TOK = 192
FEAT = 640
HALF = FEAT // 2
RB = 48
AHEAD = 3
EPSILON = 1e-05
SCALE = HD ** (-0.5)
MESH = pl.DeviceIdType.MESH
F32 = jnp.float32
BF16 = jnp.bfloat16

NT = (((1,), (1,)), ((), ()))
NN = (((1,), (0,)), ((), ()))
TN = (((0,), (0,)), ((), ()))


def dot(a, b, dims=NN):
    return lax.dot_general(a, b, dims, preferred_element_type=F32)


def fused_kernel(
    h_hbm, gain_hbm, w_hbm, q_hbm, g_hbm,
    qg_v, wg_v, gx, ng_v,
    h_v, gain_v, w_v, q_v, g_v,
    ss, ngat,
    part_a, rs_a, st_a, kvb, part_b, rs_b, st_b, kvg, kvt, kvr,
    pbuf_a, dsbuf_a, pbuf_b, dsbuf_b, nf,
    xs, xr, wgb, gpair, gz,
    loc, ss_s, ss_r, ng_s, ng_r, nc_s, nc_r,
    ra_s, ra_r, aa_s, aa_r, rb_s, rb_r, ab_s, ab_r,
    kt_s, ku_s, kt_r, x_s, x_r, az_s, az_r, cc_s, cc_r,
    gp_s, gp_r, gz_s, gz_r, gx_s, gx_r,
):
    dp = lax.axis_index("dp")
    sec = lax.axis_index("section")
    core = lax.rem(dp, 2)
    zz = lax.rem(lax.div(dp, 2), NZ)
    xh = lax.div(dp, 2 * NZ)
    yy = lax.div(sec, 2)
    xl = lax.rem(sec, 2)

    def dp_of(x_, z_, c_):
        return x_ * (2 * NZ) + z_ * 2 + c_

    sec_peer = [None] + [lax.rem(sec + o, NSEC) for o in range(1, NSEC)]
    z_at = [lax.rem(zz + o, NZ) for o in range(NZ)]
    sec_dev = [None] + [(dp, sec_peer[o]) for o in range(1, NSEC)]
    z_dev = [None] + [(dp_of(xh, z_at[o], core), sec) for o in range(1, NZ)]
    z_dev2 = [(dp_of(xh, z_at[o], 1 - core), sec) for o in range(NZ)]
    core_dev = z_dev2[0]
    x_dev = (dp_of(1 - xh, zz, core), sec)

    def rcopy(src, dst, s, r, dev):
        return pltpu.make_async_remote_copy(
            src_ref=src, dst_ref=dst, send_sem=s, recv_sem=r, device_id=dev, device_id_type=MESH
        )

    def wait_bytes(ref, sem):
        pltpu.make_async_copy(ref, ref, sem).wait()

    sends = []

    def start(c):
        c.start()
        sends.append(c.wait_send)

    def send_total(ref, sem):
        sends.append(lambda: wait_bytes(ref, sem))

    loads = [
        pltpu.make_async_copy(src, dst, loc.at[i])
        for i, (src, dst) in enumerate(
            [(h_hbm, h_v), (gain_hbm, gain_v.at[0]), (w_hbm, w_v), (q_hbm, q_v), (g_hbm, g_v)]
        )
    ]
    for c in loads:
        c.start()
    bar = pltpu.get_barrier_semaphore()
    partners = sec_dev[1:] + z_dev[1:] + z_dev2 + [x_dev]
    for dev in partners:
        pl.semaphore_signal(bar, inc=1, device_id=dev, device_id_type=MESH)

    loads[0].wait()
    acc = None
    for t in range(5):
        ht = h_v[:, t * 128:(t + 1) * 128].astype(F32)
        acc = ht * ht if acc is None else acc + ht * ht
    row = jnp.sum(acc.T, axis=0, keepdims=True)
    ss[0] = row
    pl.semaphore_wait(bar, len(partners))
    for o in range(1, NSEC):
        rcopy(ss.at[0], ss.at[o], ss_s.at[0], ss_r.at[0], sec_dev[o]).start()
    send_total(ss.at[1:NSEC], ss_s.at[0])
    loads[1].wait()
    loads[2].wait()
    wait_bytes(ss.at[1:NSEC], ss_r.at[0])
    tot = ss[0]
    for o in range(1, NSEC):
        tot = tot + ss[o]
    inv_row = lax.rsqrt(tot / D + EPSILON)
    inv = jnp.broadcast_to(inv_row, (128, TOK)).T
    for t in range(5):
        cols = slice(t * 128, (t + 1) * 128)
        n_t = (h_v[:, cols].astype(F32) * inv * gain_v[:, cols]).astype(BF16)
        ngat[core, zz, :, cols] = n_t

    my_rows = pl.ds(pl.multiple_of(yy * RB, RB), RB)

    def scatter(j, part, rs, s, r):
        for o in range(1, NSEC):
            d = sec_peer[o]
            rcopy(
                part.at[j, lax.rem(d, 2), pl.ds(pl.multiple_of(lax.div(d, 2) * RB, RB), RB), :],
                rs.at[j, o - 1], s.at[j], r.at[j], sec_dev[o],
            ).start()
        send_total(rs.at[j], s.at[j])

    def reduce_and_gather(j, part, rs, rs_r, st, dst, s, r):
        wait_bytes(rs.at[j], rs_r.at[j])
        tot = part[j, xl, my_rows, :]
        for o in range(1, NSEC):
            tot = tot + rs[j, o - 1]
        st[j] = tot.astype(BF16)
        piece = dst.at[j, xl, my_rows, :]
        for o in range(1, NSEC):
            rcopy(st.at[j], piece, s.at[j], r.at[j], sec_dev[o]).start()
        pltpu.make_async_copy(st.at[j], piece, r.at[j]).start()
        send_total(rs.at[j, :, 0:RB // 2, :], s.at[j])

    def weight_cols(j):
        return jnp.concatenate(
            [w_v[:, j * 128:(j + 1) * 128], w_v[:, 512 + j * 128:512 + (j + 1) * 128]], axis=1
        )

    def do_s(j):
        pj = dot(ngat[core, zz], weight_cols(j))
        part_a[j, 0] = pj[:, 0:128]
        part_a[j, 1] = pj[:, 128:256]
        scatter(j, part_a, rs_a, ra_s, ra_r)

    for j in range(AHEAD):
        do_s(j)
    def ring(j, d):
        sign = 1 if d == 0 else -1
        hops = 4 if (j + d) % 2 == 0 else 3
        slot0 = 0 if d == 0 else (3 if j % 2 else 4)
        return sign, hops, slot0

    ng_c = {}

    def do_ng(s, h):
        rows = pl.ds(h * 96, 96)
        if s == 0:
            own = ngat.at[core, zz, rows]
            rcopy(own, own, nc_s.at[0], nc_r.at[0], core_dev).start()
        for d in range(2):
            sign, hops, slot0 = ring(h, d)
            piece = ngat.at[core, z_at[(-sign * s) % NZ], rows]
            if 0 < s <= hops:
                ng_c[h, d, s - 1].wait_recv()
            if s < hops:
                c = rcopy(piece, piece, ng_s.at[0], ng_r.at[h, slot0 + s], z_dev[sign % NZ])
                c.start()
                ng_c[h, d, s] = c
            if 0 < s <= hops:
                rcopy(piece, piece, nc_s.at[0], nc_r.at[0], core_dev).start()

    do_ng(0, 0)
    do_ng(0, 1)
    send_total(ngat.at[0, 1:NZ], ng_s.at[0])
    send_total(ngat.at[0], nc_s.at[0])
    loads[3].wait()
    loads[4].wait()

    def do_r(j):
        reduce_and_gather(j, part_a, rs_a, ra_r, st_a, kvb, aa_s, aa_r)

    mask_a = (
        lax.broadcasted_iota(jnp.int32, (128, 128), 0)
        <= lax.broadcasted_iota(jnp.int32, (128, 128), 1)
    )
    qpos = lax.broadcasted_iota(jnp.int32, (64, 128), 1)
    mask_b = lax.broadcasted_iota(jnp.int32, (64, 128), 0) <= jnp.where(qpos < 64, qpos, qpos - 64)

    def soft(s, dpr):
        m = jnp.max(s, axis=0, keepdims=True)
        e = jnp.exp(s - m)
        p = e * (1.0 / jnp.sum(e, axis=0, keepdims=True))
        inner = jnp.sum(p * dpr, axis=0, keepdims=True)
        return p.astype(BF16), (p * (dpr - inner)).astype(BF16)

    def do_t(j):
        wait_bytes(kvb.at[j], aa_r.at[j])
        k = kvb[j, 0]
        v = kvb[j, 1]
        k_lo = k[0:128]
        v_lo = v[0:128]
        col0 = j * GRP * HD

        def heads(ref, rows, hs):
            return [ref[rows, col0 + h * HD:col0 + (h + 1) * HD] for h in hs]

        lo, hi = slice(0, 128), slice(128, TOK)
        for h in range(GRP):
            qh = heads(q_v, lo, [h])[0]
            gh = heads(g_v, lo, [h])[0]
            s = jnp.where(mask_a, dot(k_lo, qh, NT) * SCALE, -1e30)
            p, ds = soft(s, dot(v_lo, gh, NT))
            pbuf_a[:, h * 128:(h + 1) * 128] = p
            dsbuf_a[:, h * 128:(h + 1) * 128] = ds
        q_hi = jnp.concatenate(heads(q_v, hi, range(GRP)) + heads(q_v, hi, [GRP - 1]), axis=0)
        g_hi = jnp.concatenate(heads(g_v, hi, range(GRP)) + heads(g_v, hi, [GRP - 1]), axis=0)
        for i in range(3):
            qh = q_hi[i * 128:(i + 1) * 128]
            gh = g_hi[i * 128:(i + 1) * 128]
            s = dot(k, qh, NT) * SCALE
            s = jnp.concatenate([s[0:128], jnp.where(mask_b, s[128:TOK], -1e30)], axis=0)
            p, ds = soft(s, dot(v, gh, NT))
            pbuf_b[:, i * 128:(i + 1) * 128] = p
            dsbuf_b[:, i * 128:(i + 1) * 128] = ds
        q_lo = jnp.concatenate(heads(q_v, lo, range(GRP)), axis=0)
        g_lo = jnp.concatenate(heads(g_v, lo, range(GRP)), axis=0)
        nb = 64 * GRP
        kb = dot(dsbuf_b[:, 0:nb], q_hi[0:nb])
        vb = dot(pbuf_b[:, 0:nb], g_hi[0:nb])
        ka = dot(dsbuf_a[...], q_lo)
        va = dot(pbuf_a[...], g_lo)
        part_b[j, 0, 0:128] = (ka + kb[0:128]) * SCALE
        part_b[j, 0, 128:TOK] = kb[128:TOK] * SCALE
        part_b[j, 1, 0:128] = va + vb[0:128]
        part_b[j, 1, 128:TOK] = vb[128:TOK]
        scatter(j, part_b, rs_b, rb_s, rb_r)
        qa = dot(dsbuf_a[...], k_lo, TN) * SCALE
        qb = dot(dsbuf_b[:, 0:nb], k, TN) * SCALE
        for h in range(GRP):
            qg_v[0:128, col0 + h * HD:col0 + (h + 1) * HD] = qa[h * 128:(h + 1) * 128].astype(BF16)
            qg_v[128:TOK, col0 + h * HD:col0 + (h + 1) * HD] = qb[h * 64:(h + 1) * 64].astype(BF16)

    def do_u(j):
        reduce_and_gather(j, part_b, rs_b, rb_r, st_b, kvg, ab_s, ab_r)

    def do_x(j):
        wait_bytes(kvg.at[j], ab_r.at[j])
        for kv in range(2):
            turned = kvg[j, kv].T
            for z in range(NZ):
                kvt[j, kv, z] = turned[z * 16:(z + 1) * 16]
        slot = kvr.at[j, core, zz]
        for o in range(1, NZ):
            rcopy(kvt.at[j, core, z_at[o]], slot, kt_s.at[j], kt_r.at[j], z_dev[o]).start()
        for o in range(NZ):
            rcopy(kvt.at[j, 1 - core, z_at[o]], slot, ku_s.at[j], kt_r.at[j], z_dev2[o]).start()
        pltpu.make_async_copy(kvt.at[j, core, zz], slot, kt_r.at[j]).start()
        send_total(kvr.at[j, 0, 1:NZ], kt_s.at[j])
        send_total(kvr.at[j, 0], ku_s.at[j])

    x_c = {}

    def do_k(j):
        if j == 0:
            wait_bytes(ngat.at[0], nc_r.at[0])
        wait_bytes(kvr.at[j], kt_r.at[j])
        tot = None
        for c in range(2):
            for z in range(NZ):
                term = dot(kvr[j, c, z], ngat[c, z])
                tot = term if tot is None else tot + term
        xs[j] = tot
        c = rcopy(xs.at[j], xr.at[j], x_s.at[j], x_r.at[j], x_dev)
        start(c)
        x_c[j] = c

    def do_nf(j):
        both = jnp.concatenate([kvg[j, 0], kvg[j, 1]], axis=1)
        term = dot(both, weight_cols(j), NT)
        nf[...] = term if j == 0 else nf[...] + term

    def do_gain():
        gpair[0] = jnp.zeros((8, 128), F32)
        for t in range(5):
            cols = slice(t * 128, (t + 1) * 128)
            full = nf[:, cols]
            ng_v[:, cols] = full.astype(BF16)
            term = full * h_v[:, cols].astype(F32) * inv
            gpair[0, t:t + 1, :] = jnp.sum(term, axis=0, keepdims=True)
        c = rcopy(gpair.at[0], gpair.at[1], gp_s.at[0], gp_r.at[0], core_dev)
        start(c)
        g_c["p"] = c

    g_c = {}

    def do_gain_z():
        g_c["p"].wait_recv()
        gz[zz] = gpair[0] + gpair[1]
        for o in range(1, NZ):
            rcopy(gz.at[zz], gz.at[zz], gz_s.at[0], gz_r.at[0], z_dev[o]).start()
        send_total(gz.at[1:NZ], gz_s.at[0])

    def do_gain_x():
        wait_bytes(gz.at[1:NZ], gz_r.at[0])
        tot = gz[0]
        for i in range(1, NZ):
            tot = tot + gz[i]
        gpair[2] = tot
        c = rcopy(gpair.at[2], gpair.at[3], gx_s.at[0], gx_r.at[0], x_dev)
        start(c)
        g_c["x"] = c

    def do_gain_end():
        g_c["x"].wait_recv()
        gx[...] = (gpair[2] + gpair[3]) * (1.0 / 32.0)

    def do_g(j):
        x_c[j].wait_recv()
        wgb[core, j, zz] = ((xs[j] + xr[j]) * (1.0 / 32.0)).astype(BF16)
        piece = wgb.at[core, j, zz]
        for o, slot in ((2, 0), (NZ - 2, 1), (1, 2), (NZ - 1, 2)):
            rcopy(piece, piece, az_s.at[j], az_r.at[j, slot], z_dev[o]).start()
        send_total(wgb.at[0, j, 1:NZ], az_s.at[j])

    def do_a(j):
        for slot in range(2):
            sign = 1 - 2 * slot
            piece = wgb.at[core, j, z_at[(-2 * sign) % NZ]]
            wait_bytes(piece, az_r.at[j, slot])
            far = [2 * sign] if j % 2 == slot else []
            for o in far + [sign]:
                rcopy(piece, piece, az_s.at[j], az_r.at[j, 2], z_dev[o % NZ]).start()

    cc_c = {}

    def do_cc(j):
        wait_bytes(wgb.at[0, j, 0:5], az_r.at[j, 2])
        piece = wgb.at[core, j]
        c = rcopy(piece, piece, cc_s.at[j], cc_r.at[j], core_dev)
        start(c)
        cc_c[j] = c

    def do_out(j):
        cc_c[j].wait_recv()
        for half in range(2):
            wide = wgb[half, j].astype(F32).reshape(128, FEAT)
            wg_v[:, half * 512 + j * 128:half * 512 + (j + 1) * 128] = wide.T

    S, R, T, U, X, N, H = do_s, do_r, do_t, do_u, do_x, do_nf, do_ng
    K, G, A, C, O = do_k, do_g, do_a, do_cc, do_out
    steps = [
        (R, 0), (S, 3), (H, 1, 0), (R, 1), (H, 1, 1), (R, 2), (T, 0), (H, 2, 0), (R, 3), (T, 1),
        (H, 2, 1), (H, 3, 0), (U, 0), (T, 2), (H, 3, 1), (T, 3), (H, 4, 0), (X, 0), (U, 1), (U, 2),
        (H, 4, 1), (U, 3), (X, 1), (X, 2), (X, 3), (N, 0), (N, 1), (N, 2), (N, 3), (do_gain,),
        (K, 0), (do_gain_z,), (K, 1), (K, 2), (G, 0), (K, 3), (do_gain_x,), (G, 1), (A, 0), (G, 2),
        (A, 1), (G, 3), (A, 2), (C, 0), (A, 3), (C, 1), (O, 0), (do_gain_end,), (C, 2), (O, 1),
        (C, 3), (O, 2), (O, 3),
    ]
    for step in steps:
        step[0](*step[1:])

    for wait in sends:
        wait()


def finish_kernel(qg, wg, gx, ng, qg_out, wg_out, gg_out, ng_out, sem):
    copies = [(wg.at[i * 80:(i + 1) * 80], wg_out.at[i * 80:(i + 1) * 80]) for i in range(8)]
    copies += [(qg.at[i * 48:(i + 1) * 48], qg_out.at[i * 48:(i + 1) * 48]) for i in range(4)]
    copies += [(ng, ng_out)]
    copies += [(gx.at[t], gg_out.at[t * 128:(t + 1) * 128]) for t in range(5)]
    copies = [pltpu.make_async_copy(a, b, sem.at[i]) for i, (a, b) in enumerate(copies)]
    for c in copies:
        c.start()
    for c in copies:
        c.wait()


def shards(hidden, norm_gain, kv_weight, queries, out_grad):
    hbm = pl.BlockSpec(memory_space=pltpu.HBM)
    in_vmem = pl.BlockSpec(memory_space=pltpu.VMEM)
    dma = pltpu.SemaphoreType.DMA
    vm = pltpu.VMEM
    scratch = [
        vm((TOK, FEAT), BF16), vm((1, FEAT), F32), vm((FEAT, 1024), BF16),
        vm((TOK, QH * HD), BF16), vm((TOK, QH * HD), BF16),
        vm((NSEC, 1, TOK), F32), vm((2, NZ, TOK, FEAT), BF16),
        vm((KVH, 2, TOK, HD), F32), vm((KVH, 7, RB, HD), F32), vm((KVH, RB, HD), BF16),
        vm((KVH, 2, TOK, HD), BF16),
        vm((KVH, 2, TOK, HD), F32), vm((KVH, 7, RB, HD), F32), vm((KVH, RB, HD), BF16),
        vm((KVH, 2, TOK, HD), BF16), vm((KVH, 2, NZ, 16, TOK), BF16), vm((KVH, 2, NZ, 16, TOK), BF16),
        vm((128, 640), BF16), vm((128, 640), BF16), vm((TOK, 384), BF16), vm((TOK, 384), BF16),
        vm((TOK, FEAT), F32),
        vm((KVH, 16, FEAT), F32), vm((KVH, 16, FEAT), F32), vm((2, KVH, NZ, 16, FEAT), BF16),
        vm((4, 8, 128), F32), vm((NZ, 8, 128), F32),
        dma((5,)), dma((1,)), dma((1,)), dma((1,)), dma((2, 7)), dma((1,)), dma((1,)),
        dma((KVH,)), dma((KVH,)), dma((KVH,)), dma((KVH,)),
        dma((KVH,)), dma((KVH,)), dma((KVH,)), dma((KVH,)),
        dma((KVH,)), dma((KVH,)), dma((KVH,)), dma((KVH,)), dma((KVH,)),
        dma((KVH,)), dma((KVH, 3)), dma((KVH,)), dma((KVH,)),
        dma((1,)), dma((1,)), dma((1,)), dma((1,)), dma((1,)), dma((1,)),
    ]
    held = pl.pallas_call(
        fused_kernel,
        out_shape=(
            vm((TOK, QH * HD), BF16),
            vm((FEAT, 1024), F32),
            vm((8, 128), F32),
            vm((TOK, FEAT), BF16),
        ),
        in_specs=[hbm] * 5,
        out_specs=(in_vmem,) * 4,
        scratch_shapes=scratch,
        compiler_params=pltpu.CompilerParams(
            collective_id=0, has_side_effects=True, vmem_limit_bytes=40 * 1024 * 1024
        ),
        name="fused",
    )(*[pltpu.with_memory_space_constraint(a, pltpu.HBM) for a in (hidden, norm_gain, kv_weight, queries, out_grad)])
    query_grad, weight_grad, gain_grad, normed_grad = pl.pallas_call(
        finish_kernel,
        out_shape=(
            jax.ShapeDtypeStruct((TOK, QH * HD), BF16),
            jax.ShapeDtypeStruct((FEAT, 1024), F32),
            jax.ShapeDtypeStruct((FEAT,), F32),
            jax.ShapeDtypeStruct((TOK, FEAT), BF16),
        ),
        in_specs=[in_vmem] * 4,
        out_specs=(hbm,) * 4,
        scratch_shapes=[dma((18,))],
        compiler_params=pltpu.CompilerParams(vmem_limit_bytes=1024 * 1024),
        name="finish",
    )(*[pltpu.with_memory_space_constraint(a, pltpu.VMEM) for a in held])
    return query_grad, weight_grad, gain_grad, normed_grad


def solution(mesh):
    placed = (
        P("dp", "section"),
        P("section"),
        P("section", None),
        P("dp", "section"),
        P("dp", "section"),
    )
    return jax.shard_map(
        shards,
        mesh=mesh,
        in_specs=placed,
        out_specs=(P("dp", "section"), P("section", None), P("section"), P("dp", "section")),
        check_vma=False,
    )
```

```python
import jax
import jax.numpy as jnp
from jax import lax
from jax.experimental import pallas as pl
from jax.experimental.pallas import tpu as pltpu
from jax.sharding import PartitionSpec as P

D = 5120
HD = 128
KVH = 4
QH = 20
GRP = QH // KVH
NSEC = 8
NZ = 8
TOK = 192
FEAT = 640
HALF = FEAT // 2
RB = 48
AHEAD = 3
EPSILON = 1e-05
SCALE = HD ** (-0.5)
MESH = pl.DeviceIdType.MESH
F32 = jnp.float32
BF16 = jnp.bfloat16

NT = (((1,), (1,)), ((), ()))
NN = (((1,), (0,)), ((), ()))
TN = (((0,), (0,)), ((), ()))


def dot(a, b, dims=NN):
    return lax.dot_general(a, b, dims, preferred_element_type=F32)


def fused_kernel(
    h_hbm, gain_hbm, w_hbm, q_hbm, g_hbm,
    qg_v, wg_v, gx, ng_v,
    h_v, gain_v, w_v, q_v, g_v,
    ss, ngat,
    part_a, rs_a, st_a, kvb, part_b, rs_b, st_b, kvg, kvt, kvr,
    pbuf_a, dsbuf_a, pbuf_b, dsbuf_b, nf,
    xs, xr, wgb, gpair, gz,
    loc, ss_s, ss_r, ng_s, ng_r, nc_s, nc_r,
    ra_s, ra_r, aa_s, aa_r, rb_s, rb_r, ab_s, ab_r,
    kt_s, ku_s, kt_r, x_s, x_r, az_s, az_r, cc_s, cc_r,
    gp_s, gp_r, gz_s, gz_r, gx_s, gx_r,
):
    dp = lax.axis_index("dp")
    sec = lax.axis_index("section")
    core = lax.rem(dp, 2)
    zz = lax.rem(lax.div(dp, 2), NZ)
    xh = lax.div(dp, 2 * NZ)
    yy = lax.div(sec, 2)
    xl = lax.rem(sec, 2)

    def dp_of(x_, z_, c_):
        return x_ * (2 * NZ) + z_ * 2 + c_

    sec_peer = [None] + [lax.rem(sec + o, NSEC) for o in range(1, NSEC)]
    z_at = [lax.rem(zz + o, NZ) for o in range(NZ)]
    sec_dev = [None] + [(dp, sec_peer[o]) for o in range(1, NSEC)]
    z_dev = [None] + [(dp_of(xh, z_at[o], core), sec) for o in range(1, NZ)]
    z_dev2 = [(dp_of(xh, z_at[o], 1 - core), sec) for o in range(NZ)]
    core_dev = z_dev2[0]
    x_dev = (dp_of(1 - xh, zz, core), sec)

    def rcopy(src, dst, s, r, dev):
        return pltpu.make_async_remote_copy(
            src_ref=src, dst_ref=dst, send_sem=s, recv_sem=r, device_id=dev, device_id_type=MESH
        )

    def wait_bytes(ref, sem):
        pltpu.make_async_copy(ref, ref, sem).wait()

    sends = []

    def start(c):
        c.start()
        sends.append(c.wait_send)

    def send_total(ref, sem):
        sends.append(lambda: wait_bytes(ref, sem))

    loads = [
        pltpu.make_async_copy(src, dst, loc.at[i])
        for i, (src, dst) in enumerate(
            [(h_hbm, h_v), (gain_hbm, gain_v.at[0]), (w_hbm, w_v), (q_hbm, q_v), (g_hbm, g_v)]
        )
    ]
    for c in loads:
        c.start()
    bar = pltpu.get_barrier_semaphore()
    partners = sec_dev[1:] + z_dev[1:] + z_dev2 + [x_dev]
    for dev in partners:
        pl.semaphore_signal(bar, inc=1, device_id=dev, device_id_type=MESH)

    loads[0].wait()
    acc = None
    for t in range(5):
        ht = h_v[:, t * 128:(t + 1) * 128].astype(F32)
        acc = ht * ht if acc is None else acc + ht * ht
    row = jnp.sum(acc.T, axis=0, keepdims=True)
    ss[0] = row
    pl.semaphore_wait(bar, len(partners))
    for o in range(1, NSEC):
        rcopy(ss.at[0], ss.at[o], ss_s.at[0], ss_r.at[0], sec_dev[o]).start()
    send_total(ss.at[1:NSEC], ss_s.at[0])
    loads[1].wait()
    loads[2].wait()
    wait_bytes(ss.at[1:NSEC], ss_r.at[0])
    tot = ss[0]
    for o in range(1, NSEC):
        tot = tot + ss[o]
    inv_row = lax.rsqrt(tot / D + EPSILON)
    inv = jnp.broadcast_to(inv_row, (128, TOK)).T
    for t in range(5):
        cols = slice(t * 128, (t + 1) * 128)
        n_t = (h_v[:, cols].astype(F32) * inv * gain_v[:, cols]).astype(BF16)
        ngat[core, zz, :, cols] = n_t

    my_rows = pl.ds(pl.multiple_of(yy * RB, RB), RB)

    def scatter(j, part, rs, s, r):
        for o in range(1, NSEC):
            d = sec_peer[o]
            rcopy(
                part.at[j, lax.rem(d, 2), pl.ds(pl.multiple_of(lax.div(d, 2) * RB, RB), RB), :],
                rs.at[j, o - 1], s.at[j], r.at[j], sec_dev[o],
            ).start()
        send_total(rs.at[j], s.at[j])

    def reduce_and_gather(j, part, rs, rs_r, st, dst, s, r):
        wait_bytes(rs.at[j], rs_r.at[j])
        tot = part[j, xl, my_rows, :]
        for o in range(1, NSEC):
            tot = tot + rs[j, o - 1]
        st[j] = tot.astype(BF16)
        piece = dst.at[j, xl, my_rows, :]
        for o in range(1, NSEC):
            rcopy(st.at[j], piece, s.at[j], r.at[j], sec_dev[o]).start()
        pltpu.make_async_copy(st.at[j], piece, r.at[j]).start()
        send_total(rs.at[j, :, 0:RB // 2, :], s.at[j])

    def weight_cols(j):
        return jnp.concatenate(
            [w_v[:, j * 128:(j + 1) * 128], w_v[:, 512 + j * 128:512 + (j + 1) * 128]], axis=1
        )

    def do_s(j):
        pj = dot(ngat[core, zz], weight_cols(j))
        part_a[j, 0] = pj[:, 0:128]
        part_a[j, 1] = pj[:, 128:256]
        scatter(j, part_a, rs_a, ra_s, ra_r)

    for j in range(AHEAD):
        do_s(j)
    def ring(j, d):
        sign = 1 if d == 0 else -1
        hops = 4 if (j + d) % 2 == 0 else 3
        slot0 = 0 if d == 0 else (3 if j % 2 else 4)
        return sign, hops, slot0

    ng_c = {}

    def do_ng(s, h):
        rows = pl.ds(h * 96, 96)
        if s == 0:
            own = ngat.at[core, zz, rows]
            rcopy(own, own, nc_s.at[0], nc_r.at[0], core_dev).start()
        for d in range(2):
            sign, hops, slot0 = ring(h, d)
            piece = ngat.at[core, z_at[(-sign * s) % NZ], rows]
            if 0 < s <= hops:
                ng_c[h, d, s - 1].wait_recv()
            if s < hops:
                c = rcopy(piece, piece, ng_s.at[0], ng_r.at[h, slot0 + s], z_dev[sign % NZ])
                c.start()
                ng_c[h, d, s] = c
            if 0 < s <= hops:
                rcopy(piece, piece, nc_s.at[0], nc_r.at[0], core_dev).start()

    do_ng(0, 0)
    do_ng(0, 1)
    send_total(ngat.at[0, 1:NZ], ng_s.at[0])
    send_total(ngat.at[0], nc_s.at[0])
    loads[3].wait()
    loads[4].wait()

    def do_r(j):
        reduce_and_gather(j, part_a, rs_a, ra_r, st_a, kvb, aa_s, aa_r)

    mask_a = (
        lax.broadcasted_iota(jnp.int32, (128, 128), 0)
        <= lax.broadcasted_iota(jnp.int32, (128, 128), 1)
    )
    qpos = lax.broadcasted_iota(jnp.int32, (64, 128), 1)
    mask_b = lax.broadcasted_iota(jnp.int32, (64, 128), 0) <= jnp.where(qpos < 64, qpos, qpos - 64)

    def soft(s, dpr):
        m = jnp.max(s, axis=0, keepdims=True)
        e = jnp.exp(s - m)
        p = e * (1.0 / jnp.sum(e, axis=0, keepdims=True))
        inner = jnp.sum(p * dpr, axis=0, keepdims=True)
        return p.astype(BF16), (p * (dpr - inner)).astype(BF16)

    def do_t(j):
        wait_bytes(kvb.at[j], aa_r.at[j])
        k = kvb[j, 0]
        v = kvb[j, 1]
        k_lo = k[0:128]
        v_lo = v[0:128]
        col0 = j * GRP * HD

        def heads(ref, rows, hs):
            return [ref[rows, col0 + h * HD:col0 + (h + 1) * HD] for h in hs]

        lo, hi = slice(0, 128), slice(128, TOK)
        for h in range(GRP):
            qh = heads(q_v, lo, [h])[0]
            gh = heads(g_v, lo, [h])[0]
            s = jnp.where(mask_a, dot(k_lo, qh, NT) * SCALE, -1e30)
            p, ds = soft(s, dot(v_lo, gh, NT))
            pbuf_a[:, h * 128:(h + 1) * 128] = p
            dsbuf_a[:, h * 128:(h + 1) * 128] = ds
        q_hi = jnp.concatenate(heads(q_v, hi, range(GRP)) + heads(q_v, hi, [GRP - 1]), axis=0)
        g_hi = jnp.concatenate(heads(g_v, hi, range(GRP)) + heads(g_v, hi, [GRP - 1]), axis=0)
        for i in range(3):
            qh = q_hi[i * 128:(i + 1) * 128]
            gh = g_hi[i * 128:(i + 1) * 128]
            s = dot(k, qh, NT) * SCALE
            s = jnp.concatenate([s[0:128], jnp.where(mask_b, s[128:TOK], -1e30)], axis=0)
            p, ds = soft(s, dot(v, gh, NT))
            pbuf_b[:, i * 128:(i + 1) * 128] = p
            dsbuf_b[:, i * 128:(i + 1) * 128] = ds
        q_lo = jnp.concatenate(heads(q_v, lo, range(GRP)), axis=0)
        g_lo = jnp.concatenate(heads(g_v, lo, range(GRP)), axis=0)
        nb = 64 * GRP
        kb = dot(dsbuf_b[:, 0:nb], q_hi[0:nb])
        vb = dot(pbuf_b[:, 0:nb], g_hi[0:nb])
        ka = dot(dsbuf_a[...], q_lo)
        va = dot(pbuf_a[...], g_lo)
        part_b[j, 0, 0:128] = (ka + kb[0:128]) * SCALE
        part_b[j, 0, 128:TOK] = kb[128:TOK] * SCALE
        part_b[j, 1, 0:128] = va + vb[0:128]
        part_b[j, 1, 128:TOK] = vb[128:TOK]
        scatter(j, part_b, rs_b, rb_s, rb_r)
        qa = dot(dsbuf_a[...], k_lo, TN) * SCALE
        qb = dot(dsbuf_b[:, 0:nb], k, TN) * SCALE
        for h in range(GRP):
            qg_v[0:128, col0 + h * HD:col0 + (h + 1) * HD] = qa[h * 128:(h + 1) * 128].astype(BF16)
            qg_v[128:TOK, col0 + h * HD:col0 + (h + 1) * HD] = qb[h * 64:(h + 1) * 64].astype(BF16)

    def do_u(j):
        reduce_and_gather(j, part_b, rs_b, rb_r, st_b, kvg, ab_s, ab_r)

    def do_x(j):
        wait_bytes(kvg.at[j], ab_r.at[j])
        for kv in range(2):
            turned = kvg[j, kv].T
            for z in range(NZ):
                kvt[j, kv, z] = turned[z * 16:(z + 1) * 16]
        slot = kvr.at[j, core, zz]
        for o in range(1, NZ):
            rcopy(kvt.at[j, core, z_at[o]], slot, kt_s.at[j], kt_r.at[j], z_dev[o]).start()
        for o in range(NZ):
            rcopy(kvt.at[j, 1 - core, z_at[o]], slot, ku_s.at[j], kt_r.at[j], z_dev2[o]).start()
        pltpu.make_async_copy(kvt.at[j, core, zz], slot, kt_r.at[j]).start()
        send_total(kvr.at[j, 0, 1:NZ], kt_s.at[j])
        send_total(kvr.at[j, 0], ku_s.at[j])

    x_c = {}

    def do_k(j):
        if j == 0:
            wait_bytes(ngat.at[0], nc_r.at[0])
        wait_bytes(kvr.at[j], kt_r.at[j])
        tot = None
        for c in range(2):
            for z in range(NZ):
                term = dot(kvr[j, c, z], ngat[c, z])
                tot = term if tot is None else tot + term
        xs[j] = tot
        c = rcopy(xs.at[j], xr.at[j], x_s.at[j], x_r.at[j], x_dev)
        start(c)
        x_c[j] = c

    def do_nf(j):
        both = jnp.concatenate([kvg[j, 0], kvg[j, 1]], axis=1)
        term = dot(both, weight_cols(j), NT)
        nf[...] = term if j == 0 else nf[...] + term

    def do_gain():
        gpair[0] = jnp.zeros((8, 128), F32)
        for t in range(5):
            cols = slice(t * 128, (t + 1) * 128)
            full = nf[:, cols]
            ng_v[:, cols] = full.astype(BF16)
            term = full * h_v[:, cols].astype(F32) * inv
            gpair[0, t:t + 1, :] = jnp.sum(term, axis=0, keepdims=True)
        c = rcopy(gpair.at[0], gpair.at[1], gp_s.at[0], gp_r.at[0], core_dev)
        start(c)
        g_c["p"] = c

    g_c = {}

    def do_gain_z():
        g_c["p"].wait_recv()
        gz[zz] = gpair[0] + gpair[1]
        for o in range(1, NZ):
            rcopy(gz.at[zz], gz.at[zz], gz_s.at[0], gz_r.at[0], z_dev[o]).start()
        send_total(gz.at[1:NZ], gz_s.at[0])

    def do_gain_x():
        wait_bytes(gz.at[1:NZ], gz_r.at[0])
        tot = gz[0]
        for i in range(1, NZ):
            tot = tot + gz[i]
        gpair[2] = tot
        c = rcopy(gpair.at[2], gpair.at[3], gx_s.at[0], gx_r.at[0], x_dev)
        start(c)
        g_c["x"] = c

    def do_gain_end():
        g_c["x"].wait_recv()
        gx[...] = (gpair[2] + gpair[3]) * (1.0 / 32.0)

    def do_g(j):
        x_c[j].wait_recv()
        wgb[core, j, zz] = ((xs[j] + xr[j]) * (1.0 / 32.0)).astype(BF16)
        piece = wgb.at[core, j, zz]
        for o, slot in ((2, 0), (NZ - 2, 1), (1, 2), (NZ - 1, 2)):
            rcopy(piece, piece, az_s.at[j], az_r.at[j, slot], z_dev[o]).start()
        send_total(wgb.at[0, j, 1:NZ], az_s.at[j])

    def do_a(j):
        for slot in range(2):
            sign = 1 - 2 * slot
            piece = wgb.at[core, j, z_at[(-2 * sign) % NZ]]
            wait_bytes(piece, az_r.at[j, slot])
            far = [2 * sign] if j % 2 == slot else []
            for o in far + [sign]:
                rcopy(piece, piece, az_s.at[j], az_r.at[j, 2], z_dev[o % NZ]).start()

    cc_c = {}

    def do_cc(j):
        wait_bytes(wgb.at[0, j, 0:5], az_r.at[j, 2])
        piece = wgb.at[core, j]
        c = rcopy(piece, piece, cc_s.at[j], cc_r.at[j], core_dev)
        start(c)
        cc_c[j] = c

    def do_out(j):
        cc_c[j].wait_recv()
        for half in range(2):
            wide = wgb[half, j].astype(F32).reshape(128, FEAT)
            wg_v[:, half * 512 + j * 128:half * 512 + (j + 1) * 128] = wide.T

    S, R, T, U, X, N, H = do_s, do_r, do_t, do_u, do_x, do_nf, do_ng
    K, G, A, C, O = do_k, do_g, do_a, do_cc, do_out
    steps = [
        (R, 0), (S, 3), (H, 1, 0), (R, 1), (H, 1, 1), (R, 2), (T, 0), (H, 2, 0), (R, 3), (T, 1),
        (H, 2, 1), (T, 2), (H, 3, 0), (U, 0), (T, 3), (H, 3, 1), (U, 1), (H, 4, 0), (X, 0), (U, 2),
        (U, 3), (H, 4, 1), (X, 1), (X, 2), (X, 3), (K, 0), (K, 1), (N, 0), (N, 1), (N, 2),
        (N, 3), (do_gain,), (K, 2), (G, 0), (do_gain_z,), (K, 3), (G, 1), (G, 2), (A, 0), (G, 3),
        (A, 1), (do_gain_x,), (A, 2), (C, 0), (A, 3), (C, 1), (O, 0), (C, 2), (O, 1), (do_gain_end,),
        (C, 3), (O, 2), (O, 3),
    ]
    for step in steps:
        step[0](*step[1:])

    for wait in sends:
        wait()


def finish_kernel(qg, wg, gx, ng, qg_out, wg_out, gg_out, ng_out, sem):
    copies = [(wg.at[i * 80:(i + 1) * 80], wg_out.at[i * 80:(i + 1) * 80]) for i in range(8)]
    copies += [(qg.at[i * 48:(i + 1) * 48], qg_out.at[i * 48:(i + 1) * 48]) for i in range(4)]
    copies += [(ng, ng_out)]
    copies += [(gx.at[t], gg_out.at[t * 128:(t + 1) * 128]) for t in range(5)]
    copies = [pltpu.make_async_copy(a, b, sem.at[i]) for i, (a, b) in enumerate(copies)]
    for c in copies:
        c.start()
    for c in copies:
        c.wait()


def shards(hidden, norm_gain, kv_weight, queries, out_grad):
    hbm = pl.BlockSpec(memory_space=pltpu.HBM)
    in_vmem = pl.BlockSpec(memory_space=pltpu.VMEM)
    dma = pltpu.SemaphoreType.DMA
    vm = pltpu.VMEM
    scratch = [
        vm((TOK, FEAT), BF16), vm((1, FEAT), F32), vm((FEAT, 1024), BF16),
        vm((TOK, QH * HD), BF16), vm((TOK, QH * HD), BF16),
        vm((NSEC, 1, TOK), F32), vm((2, NZ, TOK, FEAT), BF16),
        vm((KVH, 2, TOK, HD), F32), vm((KVH, 7, RB, HD), F32), vm((KVH, RB, HD), BF16),
        vm((KVH, 2, TOK, HD), BF16),
        vm((KVH, 2, TOK, HD), F32), vm((KVH, 7, RB, HD), F32), vm((KVH, RB, HD), BF16),
        vm((KVH, 2, TOK, HD), BF16), vm((KVH, 2, NZ, 16, TOK), BF16), vm((KVH, 2, NZ, 16, TOK), BF16),
        vm((128, 640), BF16), vm((128, 640), BF16), vm((TOK, 384), BF16), vm((TOK, 384), BF16),
        vm((TOK, FEAT), F32),
        vm((KVH, 16, FEAT), F32), vm((KVH, 16, FEAT), F32), vm((2, KVH, NZ, 16, FEAT), BF16),
        vm((4, 8, 128), F32), vm((NZ, 8, 128), F32),
        dma((5,)), dma((1,)), dma((1,)), dma((1,)), dma((2, 7)), dma((1,)), dma((1,)),
        dma((KVH,)), dma((KVH,)), dma((KVH,)), dma((KVH,)),
        dma((KVH,)), dma((KVH,)), dma((KVH,)), dma((KVH,)),
        dma((KVH,)), dma((KVH,)), dma((KVH,)), dma((KVH,)), dma((KVH,)),
        dma((KVH,)), dma((KVH, 3)), dma((KVH,)), dma((KVH,)),
        dma((1,)), dma((1,)), dma((1,)), dma((1,)), dma((1,)), dma((1,)),
    ]
    held = pl.pallas_call(
        fused_kernel,
        out_shape=(
            vm((TOK, QH * HD), BF16),
            vm((FEAT, 1024), F32),
            vm((8, 128), F32),
            vm((TOK, FEAT), BF16),
        ),
        in_specs=[hbm] * 5,
        out_specs=(in_vmem,) * 4,
        scratch_shapes=scratch,
        compiler_params=pltpu.CompilerParams(
            collective_id=0, has_side_effects=True, vmem_limit_bytes=40 * 1024 * 1024
        ),
        name="fused",
    )(*[pltpu.with_memory_space_constraint(a, pltpu.HBM) for a in (hidden, norm_gain, kv_weight, queries, out_grad)])
    query_grad, weight_grad, gain_grad, normed_grad = pl.pallas_call(
        finish_kernel,
        out_shape=(
            jax.ShapeDtypeStruct((TOK, QH * HD), BF16),
            jax.ShapeDtypeStruct((FEAT, 1024), F32),
            jax.ShapeDtypeStruct((FEAT,), F32),
            jax.ShapeDtypeStruct((TOK, FEAT), BF16),
        ),
        in_specs=[in_vmem] * 4,
        out_specs=(hbm,) * 4,
        scratch_shapes=[dma((18,))],
        compiler_params=pltpu.CompilerParams(vmem_limit_bytes=1024 * 1024),
        name="finish",
    )(*[pltpu.with_memory_space_constraint(a, pltpu.VMEM) for a in held])
    return query_grad, weight_grad, gain_grad, normed_grad


def solution(mesh):
    placed = (
        P("dp", "section"),
        P("section"),
        P("section", None),
        P("dp", "section"),
        P("dp", "section"),
    )
    return jax.shard_map(
        shards,
        mesh=mesh,
        in_specs=placed,
        out_specs=(P("dp", "section"), P("section", None), P("section"), P("dp", "section")),
        check_vma=False,
    )
```

```python
import jax
import jax.numpy as jnp
from jax import lax
from jax.experimental import pallas as pl
from jax.experimental.pallas import tpu as pltpu
from jax.sharding import PartitionSpec as P

D = 5120
HD = 128
KVH = 4
QH = 20
GRP = QH // KVH
NSEC = 8
NZ = 8
TOK = 192
FEAT = 640
HALF = FEAT // 2
RB = 48
AHEAD = 3
SEC_FAR = (3, 5, 4, 1, 7, 2, 6)
Z_FAR = (4, 3, 5, 2, 6, 1, 7)
EPSILON = 1e-05
SCALE = HD ** (-0.5)
MESH = pl.DeviceIdType.MESH
F32 = jnp.float32
BF16 = jnp.bfloat16

NT = (((1,), (1,)), ((), ()))
NN = (((1,), (0,)), ((), ()))
TN = (((0,), (0,)), ((), ()))


def dot(a, b, dims=NN):
    return lax.dot_general(a, b, dims, preferred_element_type=F32)


def fused_kernel(
    h_hbm, gain_hbm, w_hbm, q_hbm, g_hbm,
    qg_v, wg_v, gx, ng_v,
    h_v, gain_v, w_v, q_v, g_v,
    ss, ngat,
    part_a, rs_a, st_a, kvb, part_b, rs_b, st_b, kvg, kvt, kvr,
    pbuf_a, dsbuf_a, pbuf_b, dsbuf_b, nf,
    xs, xr, wgb, gpair, gz,
    loc, ss_s, ss_r, ng_s, ng_r, nc_s, nc_r,
    ra_s, ra_r, aa_s, aa_r, rb_s, rb_r, ab_s, ab_r,
    kt_s, ku_s, kt_r, x_s, x_r, az_s, az_r, cc_s, cc_r,
    gp_s, gp_r, gz_s, gz_r, gx_s, gx_r,
):
    dp = lax.axis_index("dp")
    sec = lax.axis_index("section")
    core = lax.rem(dp, 2)
    zz = lax.rem(lax.div(dp, 2), NZ)
    xh = lax.div(dp, 2 * NZ)
    yy = lax.div(sec, 2)
    xl = lax.rem(sec, 2)

    def dp_of(x_, z_, c_):
        return x_ * (2 * NZ) + z_ * 2 + c_

    sec_peer = [None] + [lax.rem(sec + o, NSEC) for o in range(1, NSEC)]
    z_at = [lax.rem(zz + o, NZ) for o in range(NZ)]
    sec_dev = [None] + [(dp, sec_peer[o]) for o in range(1, NSEC)]
    z_dev = [None] + [(dp_of(xh, z_at[o], core), sec) for o in range(1, NZ)]
    z_dev2 = [(dp_of(xh, z_at[o], 1 - core), sec) for o in range(NZ)]
    core_dev = z_dev2[0]
    x_dev = (dp_of(1 - xh, zz, core), sec)

    def rcopy(src, dst, s, r, dev):
        return pltpu.make_async_remote_copy(
            src_ref=src, dst_ref=dst, send_sem=s, recv_sem=r, device_id=dev, device_id_type=MESH
        )

    def wait_bytes(ref, sem):
        pltpu.make_async_copy(ref, ref, sem).wait()

    sends = []

    def start(c):
        c.start()
        sends.append(c.wait_send)

    def send_total(ref, sem):
        sends.append(lambda: wait_bytes(ref, sem))

    loads = [
        pltpu.make_async_copy(src, dst, loc.at[i])
        for i, (src, dst) in enumerate(
            [(h_hbm, h_v), (gain_hbm, gain_v.at[0]), (w_hbm, w_v), (q_hbm, q_v), (g_hbm, g_v)]
        )
    ]
    for c in loads:
        c.start()
    bar = pltpu.get_barrier_semaphore()
    partners = sec_dev[1:] + z_dev[1:] + z_dev2 + [x_dev]
    for dev in partners:
        pl.semaphore_signal(bar, inc=1, device_id=dev, device_id_type=MESH)

    loads[0].wait()
    acc = None
    for t in range(5):
        ht = h_v[:, t * 128:(t + 1) * 128].astype(F32)
        acc = ht * ht if acc is None else acc + ht * ht
    row = jnp.sum(acc.T, axis=0, keepdims=True)
    ss[0] = row
    pl.semaphore_wait(bar, len(partners))
    for o in SEC_FAR:
        rcopy(ss.at[0], ss.at[o], ss_s.at[0], ss_r.at[0], sec_dev[o]).start()
    send_total(ss.at[1:NSEC], ss_s.at[0])
    loads[1].wait()
    loads[2].wait()
    wait_bytes(ss.at[1:NSEC], ss_r.at[0])
    tot = ss[0]
    for o in range(1, NSEC):
        tot = tot + ss[o]
    inv_row = lax.rsqrt(tot / D + EPSILON)
    inv = jnp.broadcast_to(inv_row, (128, TOK)).T
    for t in range(5):
        cols = slice(t * 128, (t + 1) * 128)
        n_t = (h_v[:, cols].astype(F32) * inv * gain_v[:, cols]).astype(BF16)
        ngat[core, zz, :, cols] = n_t

    my_rows = pl.ds(pl.multiple_of(yy * RB, RB), RB)

    def scatter(j, part, rs, s, r):
        for o in SEC_FAR:
            d = sec_peer[o]
            rcopy(
                part.at[j, lax.rem(d, 2), pl.ds(pl.multiple_of(lax.div(d, 2) * RB, RB), RB), :],
                rs.at[j, o - 1], s.at[j], r.at[j], sec_dev[o],
            ).start()
        send_total(rs.at[j], s.at[j])

    def reduce_and_gather(j, part, rs, rs_r, st, dst, s, r):
        wait_bytes(rs.at[j], rs_r.at[j])
        tot = part[j, xl, my_rows, :]
        for o in range(1, NSEC):
            tot = tot + rs[j, o - 1]
        st[j] = tot.astype(BF16)
        piece = dst.at[j, xl, my_rows, :]
        for o in SEC_FAR:
            rcopy(st.at[j], piece, s.at[j], r.at[j], sec_dev[o]).start()
        pltpu.make_async_copy(st.at[j], piece, r.at[j]).start()
        send_total(rs.at[j, :, 0:RB // 2, :], s.at[j])

    def weight_cols(j):
        return jnp.concatenate(
            [w_v[:, j * 128:(j + 1) * 128], w_v[:, 512 + j * 128:512 + (j + 1) * 128]], axis=1
        )

    def do_s(j):
        pj = dot(ngat[core, zz], weight_cols(j))
        part_a[j, 0] = pj[:, 0:128]
        part_a[j, 1] = pj[:, 128:256]
        scatter(j, part_a, rs_a, ra_s, ra_r)

    for j in range(AHEAD):
        do_s(j)
    def ring(j, d):
        sign = 1 if d == 0 else -1
        hops = 4 if (j + d) % 2 == 0 else 3
        slot0 = 0 if d == 0 else (3 if j % 2 else 4)
        return sign, hops, slot0

    ng_c = {}

    def do_ng(s, h):
        rows = pl.ds(h * 96, 96)
        if s == 0:
            own = ngat.at[core, zz, rows]
            rcopy(own, own, nc_s.at[0], nc_r.at[0], core_dev).start()
        for d in range(2):
            sign, hops, slot0 = ring(h, d)
            piece = ngat.at[core, z_at[(-sign * s) % NZ], rows]
            if 0 < s <= hops:
                ng_c[h, d, s - 1].wait_recv()
            if s < hops:
                c = rcopy(piece, piece, ng_s.at[0], ng_r.at[h, slot0 + s], z_dev[sign % NZ])
                c.start()
                ng_c[h, d, s] = c
            if 0 < s <= hops:
                rcopy(piece, piece, nc_s.at[0], nc_r.at[0], core_dev).start()

    do_ng(0, 0)
    do_ng(0, 1)
    send_total(ngat.at[0, 1:NZ], ng_s.at[0])
    send_total(ngat.at[0], nc_s.at[0])
    loads[3].wait()
    loads[4].wait()

    def do_r(j):
        reduce_and_gather(j, part_a, rs_a, ra_r, st_a, kvb, aa_s, aa_r)

    mask_a = (
        lax.broadcasted_iota(jnp.int32, (128, 128), 0)
        <= lax.broadcasted_iota(jnp.int32, (128, 128), 1)
    )
    qpos = lax.broadcasted_iota(jnp.int32, (64, 128), 1)
    mask_b = lax.broadcasted_iota(jnp.int32, (64, 128), 0) <= jnp.where(qpos < 64, qpos, qpos - 64)

    def soft(s, dpr):
        m = jnp.max(s, axis=0, keepdims=True)
        e = jnp.exp(s - m)
        p = e * (1.0 / jnp.sum(e, axis=0, keepdims=True))
        inner = jnp.sum(p * dpr, axis=0, keepdims=True)
        return p.astype(BF16), (p * (dpr - inner)).astype(BF16)

    def do_t(j):
        wait_bytes(kvb.at[j], aa_r.at[j])
        k = kvb[j, 0]
        v = kvb[j, 1]
        k_lo = k[0:128]
        v_lo = v[0:128]
        col0 = j * GRP * HD

        def heads(ref, rows, hs):
            return [ref[rows, col0 + h * HD:col0 + (h + 1) * HD] for h in hs]

        lo, hi = slice(0, 128), slice(128, TOK)
        for h in range(GRP):
            qh = heads(q_v, lo, [h])[0]
            gh = heads(g_v, lo, [h])[0]
            s = jnp.where(mask_a, dot(k_lo, qh, NT) * SCALE, -1e30)
            p, ds = soft(s, dot(v_lo, gh, NT))
            pbuf_a[:, h * 128:(h + 1) * 128] = p
            dsbuf_a[:, h * 128:(h + 1) * 128] = ds
        q_hi = jnp.concatenate(heads(q_v, hi, range(GRP)) + heads(q_v, hi, [GRP - 1]), axis=0)
        g_hi = jnp.concatenate(heads(g_v, hi, range(GRP)) + heads(g_v, hi, [GRP - 1]), axis=0)
        for i in range(3):
            qh = q_hi[i * 128:(i + 1) * 128]
            gh = g_hi[i * 128:(i + 1) * 128]
            s = dot(k, qh, NT) * SCALE
            s = jnp.concatenate([s[0:128], jnp.where(mask_b, s[128:TOK], -1e30)], axis=0)
            p, ds = soft(s, dot(v, gh, NT))
            pbuf_b[:, i * 128:(i + 1) * 128] = p
            dsbuf_b[:, i * 128:(i + 1) * 128] = ds
        q_lo = jnp.concatenate(heads(q_v, lo, range(GRP)), axis=0)
        g_lo = jnp.concatenate(heads(g_v, lo, range(GRP)), axis=0)
        nb = 64 * GRP
        kb = dot(dsbuf_b[:, 0:nb], q_hi[0:nb])
        vb = dot(pbuf_b[:, 0:nb], g_hi[0:nb])
        ka = dot(dsbuf_a[...], q_lo)
        va = dot(pbuf_a[...], g_lo)
        part_b[j, 0, 0:128] = (ka + kb[0:128]) * SCALE
        part_b[j, 0, 128:TOK] = kb[128:TOK] * SCALE
        part_b[j, 1, 0:128] = va + vb[0:128]
        part_b[j, 1, 128:TOK] = vb[128:TOK]
        scatter(j, part_b, rs_b, rb_s, rb_r)
        qa = dot(dsbuf_a[...], k_lo, TN) * SCALE
        qb = dot(dsbuf_b[:, 0:nb], k, TN) * SCALE
        for h in range(GRP):
            qg_v[0:128, col0 + h * HD:col0 + (h + 1) * HD] = qa[h * 128:(h + 1) * 128].astype(BF16)
            qg_v[128:TOK, col0 + h * HD:col0 + (h + 1) * HD] = qb[h * 64:(h + 1) * 64].astype(BF16)

    def do_u(j):
        reduce_and_gather(j, part_b, rs_b, rb_r, st_b, kvg, ab_s, ab_r)

    def do_x(j):
        wait_bytes(kvg.at[j], ab_r.at[j])
        for kv in range(2):
            turned = kvg[j, kv].T
            for z in range(NZ):
                kvt[j, kv, z] = turned[z * 16:(z + 1) * 16]
        slot = kvr.at[j, core, zz]
        for o in Z_FAR:
            rcopy(kvt.at[j, core, z_at[o]], slot, kt_s.at[j], kt_r.at[j], z_dev[o]).start()
            rcopy(kvt.at[j, 1 - core, z_at[o]], slot, ku_s.at[j], kt_r.at[j], z_dev2[o]).start()
        rcopy(kvt.at[j, 1 - core, zz], slot, ku_s.at[j], kt_r.at[j], core_dev).start()
        pltpu.make_async_copy(kvt.at[j, core, zz], slot, kt_r.at[j]).start()
        send_total(kvr.at[j, 0, 1:NZ], kt_s.at[j])
        send_total(kvr.at[j, 0], ku_s.at[j])

    x_c = {}

    def do_k(j):
        if j == 0:
            wait_bytes(ngat.at[0], nc_r.at[0])
        wait_bytes(kvr.at[j], kt_r.at[j])
        tot = None
        for c in range(2):
            for z in range(NZ):
                term = dot(kvr[j, c, z], ngat[c, z])
                tot = term if tot is None else tot + term
        xs[j] = tot
        c = rcopy(xs.at[j], xr.at[j], x_s.at[j], x_r.at[j], x_dev)
        start(c)
        x_c[j] = c

    def do_nf(j):
        both = jnp.concatenate([kvg[j, 0], kvg[j, 1]], axis=1)
        term = dot(both, weight_cols(j), NT)
        nf[...] = term if j == 0 else nf[...] + term

    def do_gain():
        gpair[0] = jnp.zeros((8, 128), F32)
        for t in range(5):
            cols = slice(t * 128, (t + 1) * 128)
            full = nf[:, cols]
            ng_v[:, cols] = full.astype(BF16)
            term = full * h_v[:, cols].astype(F32) * inv
            gpair[0, t:t + 1, :] = jnp.sum(term, axis=0, keepdims=True)
        c = rcopy(gpair.at[0], gpair.at[1], gp_s.at[0], gp_r.at[0], core_dev)
        start(c)
        g_c["p"] = c

    g_c = {}

    def do_gain_z():
        g_c["p"].wait_recv()
        gz[zz] = gpair[0] + gpair[1]
        for o in range(1, NZ):
            rcopy(gz.at[zz], gz.at[zz], gz_s.at[0], gz_r.at[0], z_dev[o]).start()
        send_total(gz.at[1:NZ], gz_s.at[0])

    def do_gain_x():
        wait_bytes(gz.at[1:NZ], gz_r.at[0])
        tot = gz[0]
        for i in range(1, NZ):
            tot = tot + gz[i]
        gpair[2] = tot
        c = rcopy(gpair.at[2], gpair.at[3], gx_s.at[0], gx_r.at[0], x_dev)
        start(c)
        g_c["x"] = c

    def do_gain_end():
        g_c["x"].wait_recv()
        gx[...] = (gpair[2] + gpair[3]) * (1.0 / 32.0)

    def do_g(j):
        x_c[j].wait_recv()
        wgb[core, j, zz] = ((xs[j] + xr[j]) * (1.0 / 32.0)).astype(BF16)
        piece = wgb.at[core, j, zz]
        for o, slot in ((2, 0), (NZ - 2, 1), (1, 2), (NZ - 1, 2)):
            rcopy(piece, piece, az_s.at[j], az_r.at[j, slot], z_dev[o]).start()
        send_total(wgb.at[0, j, 1:NZ], az_s.at[j])

    def do_a(j):
        for slot in range(2):
            sign = 1 - 2 * slot
            piece = wgb.at[core, j, z_at[(-2 * sign) % NZ]]
            wait_bytes(piece, az_r.at[j, slot])
            far = [2 * sign] if j % 2 == slot else []
            for o in far + [sign]:
                rcopy(piece, piece, az_s.at[j], az_r.at[j, 2], z_dev[o % NZ]).start()

    cc_c = {}

    def do_cc(j):
        wait_bytes(wgb.at[0, j, 0:5], az_r.at[j, 2])
        piece = wgb.at[core, j]
        c = rcopy(piece, piece, cc_s.at[j], cc_r.at[j], core_dev)
        start(c)
        cc_c[j] = c

    def do_out(j):
        cc_c[j].wait_recv()
        for half in range(2):
            wide = wgb[half, j].astype(F32).reshape(128, FEAT)
            wg_v[:, half * 512 + j * 128:half * 512 + (j + 1) * 128] = wide.T

    S, R, T, U, X, N, H = do_s, do_r, do_t, do_u, do_x, do_nf, do_ng
    K, G, A, C, O = do_k, do_g, do_a, do_cc, do_out
    steps = [
        (R, 0), (S, 3), (H, 1, 0), (R, 1), (H, 1, 1), (R, 2), (T, 0), (H, 2, 0), (R, 3), (T, 1),
        (H, 2, 1), (T, 2), (H, 3, 0), (U, 0), (T, 3), (H, 3, 1), (U, 1), (H, 4, 0), (X, 0), (U, 2),
        (U, 3), (H, 4, 1), (X, 1), (X, 2), (X, 3), (K, 0), (K, 1), (N, 0), (N, 1), (N, 2),
        (N, 3), (do_gain,), (K, 2), (G, 0), (do_gain_z,), (K, 3), (G, 1), (G, 2), (A, 0), (G, 3),
        (A, 1), (do_gain_x,), (A, 2), (C, 0), (A, 3), (C, 1), (O, 0), (C, 2), (O, 1), (do_gain_end,),
        (C, 3), (O, 2), (O, 3),
    ]
    for step in steps:
        step[0](*step[1:])

    for wait in sends:
        wait()


def finish_kernel(qg, wg, gx, ng, qg_out, wg_out, gg_out, ng_out, sem):
    copies = [(wg.at[i * 80:(i + 1) * 80], wg_out.at[i * 80:(i + 1) * 80]) for i in range(8)]
    copies += [(qg.at[i * 48:(i + 1) * 48], qg_out.at[i * 48:(i + 1) * 48]) for i in range(4)]
    copies += [(ng, ng_out)]
    copies += [(gx.at[t], gg_out.at[t * 128:(t + 1) * 128]) for t in range(5)]
    copies = [pltpu.make_async_copy(a, b, sem.at[i]) for i, (a, b) in enumerate(copies)]
    for c in copies:
        c.start()
    for c in copies:
        c.wait()


def shards(hidden, norm_gain, kv_weight, queries, out_grad):
    hbm = pl.BlockSpec(memory_space=pltpu.HBM)
    in_vmem = pl.BlockSpec(memory_space=pltpu.VMEM)
    dma = pltpu.SemaphoreType.DMA
    vm = pltpu.VMEM
    scratch = [
        vm((TOK, FEAT), BF16), vm((1, FEAT), F32), vm((FEAT, 1024), BF16),
        vm((TOK, QH * HD), BF16), vm((TOK, QH * HD), BF16),
        vm((NSEC, 1, TOK), F32), vm((2, NZ, TOK, FEAT), BF16),
        vm((KVH, 2, TOK, HD), F32), vm((KVH, 7, RB, HD), F32), vm((KVH, RB, HD), BF16),
        vm((KVH, 2, TOK, HD), BF16),
        vm((KVH, 2, TOK, HD), F32), vm((KVH, 7, RB, HD), F32), vm((KVH, RB, HD), BF16),
        vm((KVH, 2, TOK, HD), BF16), vm((KVH, 2, NZ, 16, TOK), BF16), vm((KVH, 2, NZ, 16, TOK), BF16),
        vm((128, 640), BF16), vm((128, 640), BF16), vm((TOK, 384), BF16), vm((TOK, 384), BF16),
        vm((TOK, FEAT), F32),
        vm((KVH, 16, FEAT), F32), vm((KVH, 16, FEAT), F32), vm((2, KVH, NZ, 16, FEAT), BF16),
        vm((4, 8, 128), F32), vm((NZ, 8, 128), F32),
        dma((5,)), dma((1,)), dma((1,)), dma((1,)), dma((2, 7)), dma((1,)), dma((1,)),
        dma((KVH,)), dma((KVH,)), dma((KVH,)), dma((KVH,)),
        dma((KVH,)), dma((KVH,)), dma((KVH,)), dma((KVH,)),
        dma((KVH,)), dma((KVH,)), dma((KVH,)), dma((KVH,)), dma((KVH,)),
        dma((KVH,)), dma((KVH, 3)), dma((KVH,)), dma((KVH,)),
        dma((1,)), dma((1,)), dma((1,)), dma((1,)), dma((1,)), dma((1,)),
    ]
    held = pl.pallas_call(
        fused_kernel,
        out_shape=(
            vm((TOK, QH * HD), BF16),
            vm((FEAT, 1024), F32),
            vm((8, 128), F32),
            vm((TOK, FEAT), BF16),
        ),
        in_specs=[hbm] * 5,
        out_specs=(in_vmem,) * 4,
        scratch_shapes=scratch,
        compiler_params=pltpu.CompilerParams(
            collective_id=0, has_side_effects=True, vmem_limit_bytes=40 * 1024 * 1024
        ),
        name="fused",
    )(*[pltpu.with_memory_space_constraint(a, pltpu.HBM) for a in (hidden, norm_gain, kv_weight, queries, out_grad)])
    query_grad, weight_grad, gain_grad, normed_grad = pl.pallas_call(
        finish_kernel,
        out_shape=(
            jax.ShapeDtypeStruct((TOK, QH * HD), BF16),
            jax.ShapeDtypeStruct((FEAT, 1024), F32),
            jax.ShapeDtypeStruct((FEAT,), F32),
            jax.ShapeDtypeStruct((TOK, FEAT), BF16),
        ),
        in_specs=[in_vmem] * 4,
        out_specs=(hbm,) * 4,
        scratch_shapes=[dma((18,))],
        compiler_params=pltpu.CompilerParams(vmem_limit_bytes=1024 * 1024),
        name="finish",
    )(*[pltpu.with_memory_space_constraint(a, pltpu.VMEM) for a in held])
    return query_grad, weight_grad, gain_grad, normed_grad


def solution(mesh):
    placed = (
        P("dp", "section"),
        P("section"),
        P("section", None),
        P("dp", "section"),
        P("dp", "section"),
    )
    return jax.shard_map(
        shards,
        mesh=mesh,
        in_specs=placed,
        out_specs=(P("dp", "section"), P("section", None), P("section"), P("dp", "section")),
        check_vma=False,
    )
```
